32 devices in a mesh: teach: 2 (over core), dp: 16 (over z, y, x).
Axes of the slice: x: 2, y: 2, z: 4, core: 2. Of those that a mesh axis runs over, the one named last changes fastest.
Arguments:
- teacher_logits: bfloat16 [2, 4096, 5000], P('teach', 'dp'), may hold values from -18 to 400
- routes: int32 [4096, 1], P('dp'), may hold values from 0 to 31; in each aligned block of 256 rows (0 to 255, 256 to 511, ...) at most 16 rows name the same one
- agreement: int32 [4096], P('dp'), may hold values 0 or 1
- targets: int32 [4096], P('dp'), may hold values from 0 to 4999
- lengths: int32 [16], P('dp'), may hold values from 64 to 256
- student_hidden: bfloat16 [8192, 1024], P(('teach', 'dp')), may hold values from -6 to 6
- out_weight: bfloat16 [1024, 5000], replicated, may hold values from -2 to 2
- out_bias: float32 [5000], replicated, may hold values from -6 to 6
- gain: float32 [1024], replicated, may hold values from 0.5 to 1.5
Outputs:
- weight_grad: float32 [1024, 5000], P(('teach', 'dp'))
- gain_grad: float32 [1024], replicated
- bias_grad: float32 [5000], replicated
- loss: float32 [], replicated
The draws below stay inside these ranges and needn't reach their ends.
Inputs may be any that keep to these rules, and one draw needn't show every extreme that they name: `routes`: within the 256 rows of one index of dp, each student device is named at most 16 times, and some device exactly 16 times.
All inputs are finite; a program needn't handle non-finite values. No bound on the sum of `agreement` on one device may be relied on, other than what follows from the above.
Results may differ from the reference program's by a relative error of at most 0.0031.
Values may be sent and summed in bfloat16 or wider, within the bound.
No kernel may reach another device: no remote copies, remote signals or barrier semaphores. Data moves between devices by JAX's collectives and lax.ppermute only.
A program may use at most 128 MiB of HBM per device.

```python
import math
import jax
import jax.numpy as jnp
import numpy as np
from jax import lax

D = 1024
V = 5000
LMAX = 256
UT = 1
RDEV = 256
NUTT = 16
TROWS = 4096
SROWS = 8192
MOST = 16
N_TEACH = 2
N_DP = 16
DEVICES = 32


def drawn_pair(key):
    states = jnp.clip(jax.random.normal(jax.random.fold_in(key, 11), (SROWS, D), jnp.float32), -6.0, 6.0)
    weights = jnp.clip(jax.random.normal(jax.random.fold_in(key, 12), (D, V), jnp.float32), -6.0, 6.0) / math.sqrt(D)
    return (states, jnp.clip(weights, -2.0, 2.0))


def draw_student_hidden(key, part):
    states, weights = drawn_pair(key)
    return states.astype(jnp.bfloat16)


def draw_out_weight(key, part):
    states, weights = drawn_pair(key)
    return weights.astype(jnp.bfloat16)


def draw_teacher_logits(key, part):
    shape = (2, TROWS, V)
    values = jnp.clip(3.0 * jax.random.normal(jax.random.fold_in(key, 22), shape, jnp.float32), -18.0, 18.0)
    return values.astype(jnp.bfloat16)


def draw_lengths(key, part):
    utterance = jnp.arange(NUTT, dtype=jnp.int32)
    device_pos = utterance // UT
    lowest = LMAX // 4 + LMAX // 2 * device_pos // max(N_DP - 1, 1)
    values = lowest + jax.random.randint(jax.random.fold_in(key, 31), (NUTT,), 0, LMAX // 4 + 1)
    values = jnp.minimum(values, LMAX)
    values = values.at[0].set(LMAX // 4).at[NUTT - 1].set(LMAX)
    return values.astype(jnp.int32)


def plant(values, key, smallest, largest):
    place = [jax.random.randint(jax.random.fold_in(key, axis), (), 0, length) for axis, length in enumerate(values.shape)]
    widest = values.shape.index(max(values.shape))
    next_to = place[:widest] + [(place[widest] + 1) % values.shape[widest]] + place[widest + 1:]
    return values.at[tuple(place)].set(smallest).at[tuple(next_to)].set(largest)


def routed_block(stream_key, own, number, rows, number_of, top, reach, skew):
    sequence = jax.random.permutation(stream_key, number_of)
    heavy_load, ordinary = portions_of(number_of, rows * top, reach, skew, True), portions_of(number_of, rows * top, reach, skew, False)
    places = jnp.arange(number_of)

    def named(tallies, turn):
        used = int((tallies > 0).sum())
        fixed = max(1, used // 4)
        passed = fixed + (places - fixed + turn * (used - fixed)) % max(1, number_of - fixed)
        return jnp.zeros((number_of,), jnp.int32).at[sequence[jnp.where(places < fixed, places, passed)]].set(jnp.asarray(tallies, jnp.int32))

    tallies = jnp.where(number % 4 == 0, named(heavy_load, number // 4), named(ordinary, number - number // 4 - 1))
    mixed = jax.random.permutation(jax.random.fold_in(own, 3), number_of)
    giver, taker = mixed[0:number_of // 2 * 2:2], mixed[1:number_of // 2 * 2:2]
    room = jnp.minimum(tallies[giver] - 1, reach - tallies[taker]) // 2
    room = jnp.where((giver == sequence[0]) | (taker == sequence[0]) | (tallies[taker] == 0), 0, jnp.maximum(room, 0))
    passed = jax.random.randint(jax.random.fold_in(own, 4), (number_of // 2,), 0, 1 << 20) % (room + 1)
    tallies = tallies.at[giver].add(-passed).at[taker].add(passed)
    items = jnp.searchsorted(jnp.cumsum(tallies), jnp.arange(rows * top), side="right").astype(jnp.int32)
    listing = items.reshape(top, rows).T
    listing = listing[jax.random.permutation(jax.random.fold_in(own, 1), rows)]
    turn = jax.random.randint(jax.random.fold_in(own, 2), (rows, 1), 0, top)
    return jnp.take_along_axis(listing, (jnp.arange(top)[None, :] + turn) % top, axis=1)


def portions_of(amount, total, reach, lean, full):
    portions = [(1 << 20) // math.isqrt(grade ** lean) + 1 for grade in range(1, amount + 1)]
    largest = reach if full else min(reach, max(-(-total // amount), total * portions[0] // sum(portions)))
    least = 1 if total - largest >= amount - 1 else 0
    counts, surplus = [largest] + [least] * (amount - 1), total - largest - least * (amount - 1)
    while surplus > 0:
        candidates = [i for i in range(1, amount) if counts[i] < largest] or [i for i in range(1, amount) if counts[i] < reach]
        mass, remaining = sum([portions[i] for i in candidates]), surplus
        for i in candidates:
            more = min(reach - counts[i], max(1, remaining * portions[i] // mass), surplus)
            counts[i] = counts[i] + more
            surplus = surplus - more
    return np.array(counts)


def bell_draw(key, shape, scale, bound, kind=jnp.bfloat16):
    return jnp.clip(scale * jax.random.normal(key, shape, jnp.float32), -bound, bound).astype(kind)


def setup_inputs(seed: int = 0) -> dict:
    keys = jax.random.split(jax.random.key(seed), 10)
    teacher_logits = draw_teacher_logits(jax.random.fold_in(keys[9], 71), 0)
    routes_keys = jax.random.split(jax.random.fold_in(keys[1], 1), TROWS // RDEV)
    routes_turns = jax.random.permutation(jax.random.fold_in(keys[1], 3), TROWS // RDEV)
    routes = jax.vmap(lambda own, number: routed_block(jax.random.fold_in(keys[1], 2), own, number, RDEV, DEVICES, 1, MOST, 2))(routes_keys, routes_turns).reshape((TROWS, 1))
    agreement = plant((jax.random.randint(keys[2], (TROWS,), 0, 4) < 3).astype(jnp.int32), jax.random.fold_in(keys[2], 1), 0, 1)
    targets = plant(jax.random.randint(keys[3], (TROWS,), 0, V), jax.random.fold_in(keys[3], 1), 0, V - 1).astype(jnp.int32)
    lengths = draw_lengths(jax.random.fold_in(keys[9], 71), 0)
    student_hidden = draw_student_hidden(jax.random.fold_in(keys[9], 71), 0)
    out_weight = draw_out_weight(jax.random.fold_in(keys[9], 71), 0)
    out_bias = bell_draw(keys[7], (V,), 1.0, 6.0, jnp.float32)
    gain = jnp.clip(1.0 + 0.1 * jax.random.normal(keys[8], (D,), jnp.float32), 0.5, 1.5)
    return {"teacher_logits": teacher_logits, "routes": routes, "agreement": agreement, "targets": targets, "lengths": lengths, "student_hidden": student_hidden, "out_weight": out_weight, "out_bias": out_bias, "gain": gain}


EPSILON = 1e-05

def route_slots(dest_device, devices):
    onehot = (dest_device[:, None] == jnp.arange(devices, dtype=jnp.int32)[None, :]).astype(jnp.float32)
    row_ids = jnp.arange(dest_device.shape[0], dtype=jnp.int32)
    earlier = (row_ids[None, :] < row_ids[:, None]).astype(jnp.float32)
    before = jnp.dot(earlier, onehot, preferred_element_type=jnp.float32, precision=lax.Precision.HIGHEST)
    return lax.optimization_barrier(jnp.sum(before * onehot, axis=1)).astype(jnp.int32)

def live_mask(lengths_block, row_total):
    row_ids = jnp.arange(row_total, dtype=jnp.int32)
    utterance = row_ids // LMAX
    frame_pos = row_ids % LMAX
    picks = utterance[:, None] == jnp.arange(lengths_block.shape[0], dtype=jnp.int32)[None, :]
    row_length = lax.optimization_barrier(jnp.sum(jnp.where(picks, lengths_block[None, :], 0), axis=1))
    return (frame_pos < row_length).astype(jnp.float32)

def soft_targets(teacher_rows, agree_rows, target_rows, live_rows):
    probs_teacher = jax.nn.softmax(teacher_rows.astype(jnp.float32), axis=-1)
    onehot = (target_rows[:, None] == jnp.arange(probs_teacher.shape[1], dtype=jnp.int32)[None, :]).astype(jnp.float32)
    weight = (0.5 * agree_rows.astype(jnp.float32))[:, None]
    return (live_rows[:, None] * (weight * probs_teacher + 0.5 * onehot)).astype(jnp.bfloat16)

def student_forward(hidden_rows, gain, out_weight, out_bias):
    states = hidden_rows.astype(jnp.float32)
    centre = lax.optimization_barrier(jnp.mean(states, axis=1, keepdims=True))
    spread = lax.optimization_barrier(jnp.mean(jnp.square(states - centre), axis=1, keepdims=True))
    normed = (states - centre) * lax.rsqrt(spread + EPSILON)
    scaled = (normed * gain[None, :]).astype(jnp.bfloat16)
    logits = jnp.dot(scaled, out_weight, preferred_element_type=jnp.float32) + out_bias[None, :]
    return (normed, scaled, jax.nn.log_softmax(logits, axis=-1))

def combined_grads(first_soft, second_soft, log_probs):
    first_float = first_soft.astype(jnp.float32)
    second_float = second_soft.astype(jnp.float32)
    row_mass = lax.optimization_barrier(jnp.sum(first_float + second_float, axis=1, keepdims=True))
    return (row_mass * jnp.exp(log_probs) - first_float - second_float).astype(jnp.bfloat16)

def reference(teacher_logits, routes, agreement, targets, lengths, student_hidden, out_weight, out_bias, gain):
    devices = N_TEACH * N_DP
    most_slots = 2 * RDEV // devices

    def one_block(totals, block_id):
        first_row = block_id * RDEV
        dest_device = lax.dynamic_slice_in_dim(routes[:, 0], first_row, RDEV, 0)
        slot_index = route_slots(dest_device, devices)
        lengths_block = lax.dynamic_slice_in_dim(lengths, block_id * UT, UT, 0)
        live_rows = live_mask(lengths_block, RDEV)
        agree_rows = lax.dynamic_slice_in_dim(agreement, first_row, RDEV, 0)
        target_rows = lax.dynamic_slice_in_dim(targets, first_row, RDEV, 0)
        student_index = (dest_device * RDEV + block_id * most_slots + slot_index).astype(jnp.int32)
        hidden_rows = jnp.take(student_hidden, student_index, axis=0)
        normed, scaled, log_probs = student_forward(hidden_rows, gain, out_weight, out_bias)
        weight_sum, gain_sum, bias_sum, loss_sum, frame_sum = totals
        first_soft = soft_targets(lax.dynamic_slice_in_dim(teacher_logits[0], first_row, RDEV, 0), agree_rows, target_rows, live_rows)
        second_soft = soft_targets(lax.dynamic_slice_in_dim(teacher_logits[1], first_row, RDEV, 0), agree_rows, target_rows, live_rows)
        grad_rows = combined_grads(first_soft, second_soft, log_probs)
        weight_sum = weight_sum + jnp.dot(scaled.T, grad_rows, preferred_element_type=jnp.float32)
        back_rows = lax.dot_general(grad_rows, out_weight, (((1,), (1,)), ((), ())), preferred_element_type=jnp.float32)
        gain_sum = gain_sum + lax.optimization_barrier(jnp.sum(back_rows * normed, axis=0))
        bias_sum = bias_sum + lax.optimization_barrier(jnp.sum(grad_rows.astype(jnp.float32), axis=0))
        loss_sum = loss_sum - jnp.sum((first_soft.astype(jnp.float32) + second_soft.astype(jnp.float32)) * log_probs)
        frame_sum = frame_sum + jnp.sum(live_rows)
        return ((weight_sum, gain_sum, bias_sum, loss_sum, frame_sum), None)
    initial = (jnp.zeros((D, V), jnp.float32), jnp.zeros((D,), jnp.float32), jnp.zeros((V,), jnp.float32), jnp.zeros((), jnp.float32), jnp.zeros((), jnp.float32))
    totals, _ = lax.scan(one_block, initial, jnp.arange(N_DP, dtype=jnp.int32))
    weight_sum, gain_sum, bias_sum, loss_sum, frame_sum = totals
    inverse = 1.0 / frame_sum
    return (weight_sum * inverse, gain_sum * inverse, bias_sum * inverse, loss_sum * inverse)
```

```python
import jax
import jax.numpy as jnp
from jax import lax
from jax.sharding import PartitionSpec as P

LMAX = 256
EPSILON = 1e-05
LANES = 128
LOWEST = -1e30
F32 = jnp.float32
BF16 = jnp.bfloat16


def torus_factors(count):
    bits = count.bit_length() - 1
    small = bits // 3
    middle = (bits - small) // 2
    return 1 << small, 1 << middle, 1 << (bits - small - middle)


def rotation(count, stride, size, step):
    def moved(index):
        place = (index // stride) % size
        return index + ((place + step) % size - place) * stride

    return [(index, moved(index)) for index in range(count)]


def route_slots(dest_device):
    row_ids = jnp.arange(dest_device.shape[0], dtype=jnp.int32)
    same = (dest_device[:, None] == dest_device[None, :]) & (row_ids[None, :] < row_ids[:, None])
    return jnp.sum(same.astype(jnp.int32), axis=1)


def live_mask(lengths_block, row_total):
    row_ids = jnp.arange(row_total, dtype=jnp.int32)
    utterance = row_ids // LMAX
    frame_pos = row_ids % LMAX
    picks = utterance[:, None] == jnp.arange(lengths_block.shape[0], dtype=jnp.int32)[None, :]
    row_length = jnp.sum(jnp.where(picks, lengths_block[None, :], 0), axis=1)
    return (frame_pos < row_length).astype(F32)


def soft_targets(teacher_rows, agree_rows, target_rows, live_rows):
    probs_teacher = jax.nn.softmax(teacher_rows.astype(F32), axis=-1)
    onehot = (
        target_rows[:, None] == jnp.arange(probs_teacher.shape[1], dtype=jnp.int32)[None, :]
    ).astype(F32)
    weight = (0.5 * agree_rows.astype(F32))[:, None]
    return (live_rows[:, None] * (weight * probs_teacher + 0.5 * onehot)).astype(BF16)


def body(
    teacher_logits, routes, agreement, targets, lengths, student_hidden, out_weight, out_bias, gain
):
    cores = lax.axis_size("teach")
    chips = lax.axis_size("dp")
    devices = cores * chips
    rows = teacher_logits.shape[1]
    slots = cores * rows // devices
    vocab = teacher_logits.shape[2]
    width = student_hidden.shape[1]
    out_rows = width // devices
    size_a, size_b, size_c = torus_factors(chips)
    part = -(-vocab // (2 * cores * LANES)) * LANES
    half = 2 * part
    padded = cores * half
    core = lax.axis_index("teach")
    chip = lax.axis_index("dp")
    at_a = chip % size_a
    at_b = (chip // size_a) % size_b
    at_c = chip // (size_a * size_b)
    other = [(i, 1 - i) for i in range(cores)]

    def swap(value):
        return lax.ppermute(value, "teach", other)

    def along(value, stride, size, step):
        return lax.ppermute(value, "dp", rotation(chips, stride, size, step))

    def pick(whole, index):
        return jnp.where(index == 0, whole[..., :half], whole[..., half:])

    arrived = lax.all_to_all(
        student_hidden.reshape(chips, slots, width), "dp", split_axis=0, concat_axis=0, tiled=True
    ).reshape(chips * slots, width)
    arrived_other = swap(arrived)

    dest_device = routes[:, 0]
    slot_index = route_slots(dest_device)
    live_rows = live_mask(lengths, rows)
    soft_rows = soft_targets(teacher_logits[0], agreement, targets, live_rows)
    soft_rows = jnp.pad(soft_rows, ((0, 0), (0, padded - vocab)))
    soft_mine = pick(soft_rows, core)
    soft_other = swap(pick(soft_rows, 1 - core))
    soft_sum = soft_mine.astype(F32) + soft_other.astype(F32)

    weight_half = pick(jnp.pad(out_weight, ((0, 0), (0, padded - vocab))), core)
    bias_half = pick(jnp.pad(out_bias, (0, padded - vocab), constant_values=LOWEST), core)

    place = (dest_device % chips) * slots + slot_index
    ids = jnp.arange(chips * slots, dtype=jnp.int32)[None, :]
    from_core = (dest_device // chips)[:, None]
    hit = place[:, None] == ids
    hidden_rows = jnp.dot(
        (hit & (from_core == core)).astype(BF16), arrived, preferred_element_type=F32
    ) + jnp.dot(
        (hit & (from_core != core)).astype(BF16), arrived_other, preferred_element_type=F32
    )
    centre = jnp.mean(hidden_rows, axis=1, keepdims=True)
    spread = jnp.mean(jnp.square(hidden_rows - centre), axis=1, keepdims=True)
    normed = (hidden_rows - centre) * lax.rsqrt(spread + EPSILON)
    scaled = (normed * gain[None, :]).astype(BF16)

    logits = jnp.dot(scaled, weight_half, preferred_element_type=F32) + bias_half[None, :]
    top = jnp.max(logits, axis=1)
    total = jnp.sum(jnp.exp(logits - top[:, None]), axis=1)
    mass_half = jnp.sum(soft_sum, axis=1)
    stats = jnp.stack([top, total, mass_half])
    stats_other = swap(stats)
    top_all = jnp.maximum(top, stats_other[0])
    total_all = total * jnp.exp(top - top_all) + stats_other[1] * jnp.exp(stats_other[0] - top_all)
    mass = (mass_half + stats_other[2])[:, None]
    log_probs = logits - top_all[:, None] - jnp.log(total_all)[:, None]
    grad = (
        mass * jnp.exp(log_probs) - soft_mine.astype(F32) - soft_other.astype(F32)
    ).astype(BF16)
    loss_term = -jnp.sum(soft_sum * log_probs)

    by_place = scaled.reshape(rows, cores, size_c, size_b, size_a, out_rows)

    def part_of(grad_part, axis_index, near, far):
        near_at, near_stride, near_size = near
        far_at, far_stride, far_size = far
        order = (axis_index, 7 - axis_index, 2, 1, 5)
        ordered = jnp.transpose(by_place, (0,) + order).reshape(rows, near_size, -1)
        partial = None
        for step in range(near_size):
            states = lax.dynamic_index_in_dim(
                ordered, (near_at + step) % near_size, 1, keepdims=False
            )
            grads = grad_part
            if step:
                states = along(states, near_stride, near_size, step)
                grads = along(grads, near_stride, near_size, step)
            term = lax.dot_general(
                states, grads, (((0,), (0,)), ((), ())), preferred_element_type=F32
            )
            partial = term if partial is None else partial + term

        def reduced(partial, at, stride, size):
            pieces = partial.reshape(size, partial.shape[0] // size, partial.shape[1])
            kept = lax.dynamic_index_in_dim(pieces, at, 0, keepdims=False)
            for step in range(1, size):
                sent = lax.dynamic_index_in_dim(pieces, (at + step) % size, 0, keepdims=False)
                kept = kept + along(sent.astype(BF16), stride, size, step).astype(F32)
            return kept

        partial = reduced(partial, far_at, far_stride, far_size)
        return reduced(partial, at_c, size_a * size_b, size_c)

    axis_a = (at_a, 1, size_a)
    axis_b = (at_b, size_a, size_b)
    first = part_of(grad[:, :part], 4, axis_a, axis_b)
    second = part_of(grad[:, part:], 3, axis_b, axis_a)
    mine = jnp.concatenate([first, second], axis=1).reshape(cores, out_rows, half)

    back = lax.dot_general(
        grad, weight_half, (((1,), (1,)), ((), ())), preferred_element_type=F32
    )
    small = jnp.concatenate(
        [
            jnp.sum(grad.astype(F32), axis=0),
            jnp.sum(back * normed, axis=0),
            loss_term[None],
            jnp.sum(live_rows)[None],
        ]
    )
    step = 1
    while step < chips:
        small = small + lax.ppermute(small, "dp", [(i, i ^ step) for i in range(chips)])
        step *= 2
    small_other = swap(small)
    inverse = 1.0 / small[half + width + 1]
    bias_low = jnp.where(core == 0, small[:half], small_other[:half])
    bias_high = jnp.where(core == 0, small_other[:half], small[:half])
    bias_sum = jnp.concatenate([bias_low, bias_high])[:vocab]
    rest = small[half:] + small_other[half:]

    kept = lax.dynamic_index_in_dim(mine, core, 0, keepdims=False) * inverse
    got = swap(lax.dynamic_index_in_dim(mine, 1 - core, 0, keepdims=False) * inverse)
    low = jnp.where(core == 0, kept, got)
    high = jnp.where(core == 0, got, kept)
    weight_grad = jnp.concatenate([low, high], axis=1)[:, :vocab]
    return (weight_grad, rest[:width] * inverse, bias_sum * inverse, rest[width] * inverse)


def solution(mesh):
    return jax.shard_map(
        body,
        mesh=mesh,
        in_specs=(
            P("teach", "dp", None),
            P("dp", None),
            P("dp"),
            P("dp"),
            P("dp"),
            P(("teach", "dp"), None),
            P(),
            P(),
            P(),
        ),
        out_specs=(P(("teach", "dp"), None), P(), P(), P()),
        check_vma=False,
    )
```

```python
import functools

import jax
import jax.numpy as jnp
from jax import lax
from jax.experimental import pallas as pl
from jax.experimental.pallas import tpu as pltpu
from jax.sharding import PartitionSpec as P

LMAX = 256
EPSILON = 1e-05
LANES = 128
TILES = 4
LOWEST = -1e30
F32 = jnp.float32
BF16 = jnp.bfloat16


def bits_of(count):
    return count.bit_length() - 1


def torus_factors(count):
    bits = bits_of(count)
    small = bits // 3
    middle = (bits - small) // 2
    return 1 << small, 1 << middle, 1 << (bits - small - middle)


def rotation(count, stride, size, step):
    def moved(index):
        place = (index // stride) % size
        return index + ((place + step) % size - place) * stride

    return [(index, moved(index)) for index in range(count)]


def route_slots(dest_device):
    row_ids = jnp.arange(dest_device.shape[0], dtype=jnp.int32)
    same = (dest_device[:, None] == dest_device[None, :]) & (row_ids[None, :] < row_ids[:, None])
    return jnp.sum(same.astype(jnp.int32), axis=1)


def live_mask(lengths_block, row_total):
    row_ids = jnp.arange(row_total, dtype=jnp.int32)
    utterance = row_ids // LMAX
    frame_pos = row_ids % LMAX
    picks = utterance[:, None] == jnp.arange(lengths_block.shape[0], dtype=jnp.int32)[None, :]
    row_length = jnp.sum(jnp.where(picks, lengths_block[None, :], 0), axis=1)
    return (frame_pos < row_length).astype(F32)


def call(kernel, name, grid, in_specs, out_specs, out_shape, scratch=(), prefetch=1):
    return pl.pallas_call(
        kernel,
        name=name,
        grid_spec=pltpu.PrefetchScalarGridSpec(
            num_scalar_prefetch=prefetch,
            grid=grid,
            in_specs=in_specs,
            out_specs=out_specs,
            scratch_shapes=list(scratch),
        ),
        out_shape=out_shape,
        compiler_params=pltpu.CompilerParams(
            dimension_semantics=("arbitrary",) * len(grid), vmem_limit_bytes=48 << 20
        ),
    )


def shape(*dims, dtype=F32):
    return jax.ShapeDtypeStruct(dims, dtype)


def soft_kernel(half, core_ref, logits_ref, weight_ref, hot_ref, target_ref, mine_ref, other_ref, mass_ref):
    rows, vocab = logits_ref.shape
    values = logits_ref[...].astype(F32)
    values = jnp.exp(values - jnp.max(values, axis=1, keepdims=True))
    scale = weight_ref[...] / jnp.sum(values, axis=1, keepdims=True)
    pieces = lax.broadcasted_iota(jnp.int32, (rows, vocab), 1)
    hot = jnp.where(pieces == target_ref[...], hot_ref[...], 0.0)
    soft = (values * scale + hot).astype(BF16)
    mass_ref[...] = jnp.sum(soft.astype(F32), axis=1, keepdims=True)
    low = soft[:, :half]
    first = core_ref[0] == 0

    @pl.when(first)
    def _():
        mine_ref[...] = low
        other_ref[...] = jnp.zeros_like(other_ref)
        other_ref[:, : vocab - half] = soft[:, half:]

    @pl.when(jnp.logical_not(first))
    def _():
        other_ref[...] = low
        mine_ref[...] = jnp.zeros_like(mine_ref)
        mine_ref[:, : vocab - half] = soft[:, half:]


def soft_targets(core, half, logits, weight, hot, target):
    rows, vocab = logits.shape
    block = 32
    column = pl.BlockSpec((block, 1), lambda i, c: (i, 0))
    piece = pl.BlockSpec((block, half), lambda i, c: (i, 0))
    return call(
        functools.partial(soft_kernel, half),
        "soft",
        (rows // block,),
        [pl.BlockSpec((block, vocab), lambda i, c: (i, 0)), column, column, column],
        [piece, piece, column],
        [shape(rows, half, dtype=BF16), shape(rows, half, dtype=BF16), shape(rows, 1)],
    )(core, logits, weight, hot, target)


def select_kernel(place_ref, near_ref, far_ref, gain_ref, normed_ref, scaled_ref, turned_ref):
    rows = place_ref.shape[0]
    count = near_ref.shape[0]
    ids = lax.broadcasted_iota(jnp.int32, (rows, count), 1)
    place = place_ref[...]
    hidden = jnp.dot(
        (place == ids).astype(F32).astype(BF16), near_ref[...], preferred_element_type=F32
    ) + jnp.dot(
        (place - count == ids).astype(F32).astype(BF16), far_ref[...], preferred_element_type=F32
    )
    centre = jnp.mean(hidden, axis=1, keepdims=True)
    moved = hidden - centre
    spread = jnp.mean(moved * moved, axis=1, keepdims=True)
    normed = moved * lax.rsqrt(spread + EPSILON)
    scaled = normed * gain_ref[...]
    normed_ref[...] = normed
    scaled_ref[...] = scaled.astype(BF16)
    turned_ref[...] = scaled.T.astype(BF16)


def select_states(place, near, far, gain):
    rows = place.shape[0]
    width = near.shape[1]
    return pl.pallas_call(
        select_kernel,
        name="select",
        out_shape=[
            shape(rows, width),
            shape(rows, width, dtype=BF16),
            shape(width, rows, dtype=BF16),
        ],
        compiler_params=pltpu.CompilerParams(vmem_limit_bytes=48 << 20),
    )(place, near, far, gain)


def forward_kernel(
    vocab, core_ref, scaled_ref, weight_ref, bias_ref, mine_ref, other_ref,
    powers_ref, tops_ref, totals_ref, dots_ref,
):
    step = pl.program_id(0)
    rows, tile = powers_ref.shape
    start = (core_ref[0] * pl.num_programs(0) + step) * tile
    logits = jnp.dot(scaled_ref[...], weight_ref[...], preferred_element_type=F32) + bias_ref[...]
    pieces = lax.broadcasted_iota(jnp.int32, (rows, tile), 1) + start
    logits = jnp.where(pieces < vocab, logits, LOWEST)
    top = jnp.max(logits, axis=1, keepdims=True)
    powers = jnp.exp(logits - top)
    powers_ref[...] = powers
    soft = mine_ref[...].astype(F32) + other_ref[...].astype(F32)

    @pl.when(step == 0)
    def _():
        tops_ref[...] = jnp.full_like(tops_ref, LOWEST)
        totals_ref[...] = jnp.zeros_like(totals_ref)
        dots_ref[...] = jnp.zeros_like(dots_ref)

    lane = lax.broadcasted_iota(jnp.int32, tops_ref.shape, 1) == step
    tops_ref[...] = jnp.where(lane, top, tops_ref[...])
    totals_ref[...] = jnp.where(lane, jnp.sum(powers, axis=1, keepdims=True), totals_ref[...])
    dots_ref[...] += jnp.sum(soft * logits, axis=1, keepdims=True)


def student_forward(core, vocab, tile, scaled, weight, bias, mine, other):
    rows, width = scaled.shape
    last = -(-vocab // tile) - 1
    whole = pl.BlockSpec((rows, width), lambda j, c: (0, 0))
    stat = pl.BlockSpec((rows, LANES), lambda j, c: (0, 0))
    piece = pl.BlockSpec((rows, tile), lambda j, c: (0, j))

    def at(j, c):
        return (0, jnp.minimum(c[0] * TILES + j, last))

    return call(
        functools.partial(forward_kernel, vocab),
        "forward",
        (TILES,),
        [whole, pl.BlockSpec((width, tile), at), pl.BlockSpec((1, tile), at), piece, piece],
        [piece, stat, stat, pl.BlockSpec((rows, 1), lambda j, c: (0, 0))],
        [shape(rows, TILES * tile), shape(rows, LANES), shape(rows, LANES), shape(rows, 1)],
    )(core, scaled, weight, bias, mine, other)


def grad_kernel(
    tiles, step_ref, powers_ref, tops_ref, totals_ref, tops_far_ref, totals_far_ref,
    mass_ref, mass_far_ref, dots_ref, mine_ref, other_ref,
    *out_refs,
):
    step = pl.program_id(0)
    tops, tops_far = tops_ref[...], tops_far_ref[...]
    top = jnp.maximum(
        jnp.max(tops, axis=1, keepdims=True), jnp.max(tops_far, axis=1, keepdims=True)
    )
    shrunk = jnp.exp(tops - top)
    total = jnp.sum(
        totals_ref[...] * shrunk + totals_far_ref[...] * jnp.exp(tops_far - top),
        axis=1,
        keepdims=True,
    )
    mass = mass_ref[...] + mass_far_ref[...]
    at = step_ref[0] + 2 * step
    lane = lax.broadcasted_iota(jnp.int32, shrunk.shape, 1) == at
    own = jnp.sum(jnp.where(lane, shrunk, 0.0), axis=1, keepdims=True)
    scale = mass * own / total
    grad = powers_ref[...] * scale - mine_ref[...].astype(F32) - other_ref[...].astype(F32)
    grad = grad.astype(BF16)
    bias = jnp.sum(grad.astype(F32), axis=0, keepdims=True)
    for index in range(tiles):

        @pl.when(step == index)
        def _(index=index):
            out_refs[index][...] = grad
            out_refs[tiles + index][...] = bias

    loss = 0.5 * mass * (top + jnp.log(total)) - dots_ref[...]
    out_refs[2 * tiles][...] = jnp.broadcast_to(jnp.sum(loss), out_refs[2 * tiles].shape)


def combined_grads(turn, tile, powers, tops, totals, tops_far, totals_far, mass, mass_far, dots, mine, other):
    rows = powers.shape[0]
    count = TILES // 2
    stat = pl.BlockSpec((rows, LANES), lambda j, s: (0, 0))
    column = pl.BlockSpec((rows, 1), lambda j, s: (0, 0))
    piece = pl.BlockSpec((rows, tile), lambda j, s: (0, s[0] + 2 * j))
    result = call(
        functools.partial(grad_kernel, count),
        "grad",
        (count,),
        [piece, stat, stat, stat, stat, column, column, column, piece, piece],
        [pl.BlockSpec((rows, tile), lambda j, s: (0, 0))] * count
        + [pl.BlockSpec((1, tile), lambda j, s: (0, 0))] * count
        + [pl.BlockSpec((1, LANES), lambda j, s: (0, 0))],
        [shape(rows, tile, dtype=BF16)] * count + [shape(1, tile)] * count + [shape(1, LANES)],
    )(
        jnp.full((1,), turn, jnp.int32),
        powers, tops, totals, tops_far, totals_far, mass, mass_far, dots, mine, other,
    )
    return result[:count], result[count : 2 * count], result[-1][0, 0]


def back_kernel(vocab, core_ref, weight_ref, normed_ref, *refs):
    grads, (out_ref, total_ref) = refs[:TILES], refs[TILES:]
    step = pl.program_id(0)
    width, tile = weight_ref.shape
    start = (core_ref[0] * TILES + step) * tile
    pieces = lax.broadcasted_iota(jnp.int32, (width, tile), 1) + start
    weight = weight_ref[...]
    weight = jnp.where(pieces < vocab, weight, jnp.zeros_like(weight))

    @pl.when(step == 0)
    def _():
        total_ref[...] = jnp.zeros_like(total_ref)

    for index in range(TILES):

        @pl.when(step == index)
        def _(index=index):
            total_ref[...] += lax.dot_general(
                grads[index][...], weight, (((1,), (1,)), ((), ())), preferred_element_type=F32
            )

    @pl.when(step == TILES - 1)
    def _():
        out_ref[...] = jnp.sum(total_ref[...] * normed_ref[...], axis=0, keepdims=True)


def gain_term(core, vocab, weight, normed, grads):
    rows, width = normed.shape
    tile = grads[0].shape[1]
    last = -(-vocab // tile) - 1
    return call(
        functools.partial(back_kernel, vocab),
        "back",
        (TILES,),
        [
            pl.BlockSpec((width, tile), lambda j, c: (0, jnp.minimum(c[0] * TILES + j, last))),
            pl.BlockSpec((rows, width), lambda j, c: (0, 0)),
        ]
        + [pl.BlockSpec((rows, tile), lambda j, c: (0, 0))] * TILES,
        pl.BlockSpec((1, width), lambda j, c: (0, 0)),
        shape(1, width),
        [pltpu.VMEM((rows, width), F32)],
    )(core, weight, normed, *grads)


def term_kernel(near, bit_ref, *refs):
    states, grads, (kept_ref, sent_ref) = refs[:near], refs[near : 2 * near], refs[2 * near :]
    count = kept_ref.shape[0]

    def product(side):
        rows = pl.ds(pl.multiple_of(side * count, count), count)
        total = None
        for state, grad in zip(states, grads):
            term = jnp.dot(state[rows, :], grad[...], preferred_element_type=F32)
            total = term if total is None else total + term
        return total

    sent_ref[...] = product(1 - bit_ref[0]).astype(BF16)
    kept_ref[...] = product(bit_ref[0])


def weight_term(bit, states, grads):
    count = states[0].shape[0] // 2
    tile = grads[0].shape[1]
    in_specs = [pl.BlockSpec(s.shape, lambda i, b: (0, 0)) for s in (*states, *grads)]
    return call(
        functools.partial(term_kernel, len(states)),
        "term",
        (1,),
        in_specs,
        [pl.BlockSpec((count, tile), lambda i, b: (0, 0))] * 2,
        [shape(count, tile), shape(count, tile, dtype=BF16)],
    )(bit[None], *states, *grads)


def body(
    teacher_logits, routes, agreement, targets, lengths, student_hidden, out_weight, out_bias, gain
):
    cores = lax.axis_size("teach")
    chips = lax.axis_size("dp")
    devices = cores * chips
    rows = teacher_logits.shape[1]
    slots = cores * rows // devices
    vocab = teacher_logits.shape[2]
    width = student_hidden.shape[1]
    out_rows = width // devices
    size_a, size_b, size_c = torus_factors(chips)
    tile = -(-vocab // (TILES * cores * LANES)) * LANES
    half = TILES * tile
    core = lax.axis_index("teach").astype(jnp.int32)
    chip = lax.axis_index("dp").astype(jnp.int32)
    core_only = core[None]
    exchange = [(i, 1 - i) for i in range(cores)]

    def swap(value):
        return lax.ppermute(value, "teach", exchange)

    def bit_of(stride):
        return (chip // stride) % 2

    with jax.named_scope("hidden"):
        arrived = lax.all_to_all(
            student_hidden.reshape(chips, slots, width),
            "dp",
            split_axis=0,
            concat_axis=0,
            tiled=True,
        ).reshape(chips * slots, width)
    arrived_far = swap(arrived)

    dest_device = routes[:, 0]
    slot_index = route_slots(dest_device)
    live_rows = live_mask(lengths, rows)
    with jax.named_scope("teacher"):
        mine, other, mass = soft_targets(
            core_only,
            half,
            teacher_logits[0],
            (0.5 * agreement.astype(F32) * live_rows)[:, None],
            (0.5 * live_rows)[:, None],
            targets[:, None],
        )
    other = swap(other)
    mass_far = swap(mass)

    place = (dest_device % chips) * slots + slot_index
    place = jnp.where(dest_device // chips == core, place, place + chips * slots)
    normed, scaled, turned = select_states(place[:, None], arrived, arrived_far, gain[None, :])

    bits_a, bits_b, bits_c = bits_of(size_a), bits_of(size_b), bits_of(size_c)
    turned = turned.reshape((cores,) + (2,) * bits_c + (size_b, size_a, out_rows, rows))

    def states_for(axis, index):
        taken = lax.dynamic_index_in_dim(turned, index, 1 + bits_c + axis, keepdims=False)
        far_bits = bits_a if axis == 0 else bits_b
        taken = taken.reshape((cores,) + (2,) * (bits_c + far_bits) + (out_rows, rows))
        order = tuple(range(bits_c + far_bits, 0, -1)) + (0,)
        order = order[far_bits * 0 :] + (1 + bits_c + far_bits, 2 + bits_c + far_bits)
        return jnp.transpose(taken, order).reshape(-1, rows)

    def along(value, stride, size, step):
        return lax.ppermute(value, "dp", rotation(chips, stride, size, step))

    deep = [size_a * size_b << k for k in range(bits_c)]
    plans = (
        ((1, 1, size_a), [size_a << k for k in range(bits_b)] + deep),
        ((0, size_a, size_b), [1 << k for k in range(bits_a)] + deep),
    )
    states = []
    for (axis, stride, size), _ in plans:
        at = (chip // stride) % size
        gathered = []
        for step in range(size):
            piece = states_for(axis, (at + step) % size)
            gathered.append(along(piece, stride, size, step) if step else piece)
        states.append(gathered)

    powers, tops, totals, dots = student_forward(
        core_only, vocab, tile, scaled, out_weight, out_bias[None, :], mine, other
    )
    tops_far, totals_far = swap(tops), swap(totals)

    grads, biases, losses = [None] * TILES, [None] * TILES, []
    for turn in range(TILES // 2):
        made, bias, loss = combined_grads(
            turn, tile, powers, tops, totals, tops_far, totals_far, mass, mass_far, dots, mine, other
        )
        grads[turn::2] = made
        biases[turn::2] = bias
        losses.append(loss)

    gathered = {}
    for turn in range(TILES // 2):
        for side, ((axis, stride, size), _) in enumerate(plans):
            grad = grads[turn + 2 * side]
            gathered[turn, side] = [
                along(grad, stride, size, step) if step else grad for step in range(size)
            ]

    first = gathered[0, 0][-1]
    pieces = [None] * TILES
    for turn in range(TILES // 2):
        for side, (_, strides) in enumerate(plans):
            kept, sent = weight_term(bit_of(strides[0]), states[side], gathered[turn, side])
            for place, stride in enumerate(strides):
                if place:
                    halves = kept.reshape(2, kept.shape[0] // 2, tile)
                    bit = bit_of(stride)
                    sent = lax.dynamic_index_in_dim(halves, 1 - bit, 0, keepdims=False)
                    kept = lax.dynamic_index_in_dim(halves, bit, 0, keepdims=False)
                    sent = sent.astype(BF16)
                pairs = [(i, i ^ stride) for i in range(chips)]
                kept = kept + lax.ppermute(sent, "dp", pairs).astype(F32)
            pieces[turn + 2 * side] = kept.reshape(cores, out_rows, tile)

    grads_late, _ = lax.optimization_barrier((tuple(grads), first))
    small = jnp.concatenate(
        [bias[0] for bias in biases]
        + [
            gain_term(core_only, vocab, out_weight, normed, grads_late)[0],
            losses[0][None],
            jnp.sum(live_rows)[None],
        ]
    )
    for stride in deep + [1 << k for k in range(bits_a + bits_b)]:
        small = small + lax.ppermute(small, "dp", [(i, i ^ stride) for i in range(chips)])
    small_far = swap(small)
    inverse = 1.0 / small[half + width + 1]
    bias_low = jnp.where(core == 0, small[:half], small_far[:half])
    bias_high = jnp.where(core == 0, small_far[:half], small[:half])
    bias_sum = jnp.concatenate([bias_low, bias_high])[:vocab]
    rest = small[half:] + small_far[half:]

    whole = jnp.concatenate(pieces, axis=2)
    kept = lax.dynamic_index_in_dim(whole, core, 0, keepdims=False)
    got = swap(lax.dynamic_index_in_dim(whole, 1 - core, 0, keepdims=False))
    low = jnp.where(core == 0, kept, got)
    high = jnp.where(core == 0, got, kept)
    weight_grad = jnp.concatenate([low, high], axis=1)[:, :vocab]
    return (weight_grad * inverse, rest[:width] * inverse, bias_sum * inverse, rest[width] * inverse)


def solution(mesh):
    return jax.shard_map(
        body,
        mesh=mesh,
        in_specs=(
            P("teach", "dp", None),
            P("dp", None),
            P("dp"),
            P("dp"),
            P("dp"),
            P(("teach", "dp"), None),
            P(),
            P(),
            P(),
        ),
        out_specs=(P(("teach", "dp"), None), P(), P(), P()),
        check_vma=False,
    )
```

```python
import functools
import math

import jax
import jax.numpy as jnp
from jax import lax
from jax.experimental import pallas as pl
from jax.experimental.pallas import tpu as pltpu
from jax.sharding import PartitionSpec as P


LMAX = 256
EPSILON = 1e-05
LANES = 128
TURNS = 2
TILES = 2 * TURNS
F32 = jnp.float32
BF16 = jnp.bfloat16
CONTRACT_LAST = (((1,), (1,)), ((), ()))
CONTRACT_FIRST = (((0,), (0,)), ((), ()))


def bits_of(count):
    return count.bit_length() - 1


def torus_factors(count):
    bits = bits_of(count)
    small = bits // 3
    middle = (bits - small) // 2
    return 1 << small, 1 << middle, 1 << (bits - small - middle)


def rotation(count, stride, size, step):
    def moved(index):
        place = (index // stride) % size
        return index + ((place + step) % size - place) * stride

    return [(index, moved(index)) for index in range(count)]


def flips(strides):
    masks = [0]
    for stride in strides:
        masks += [mask | stride for mask in masks]
    return masks[1:]


def route_slots(dest_device):
    row_ids = jnp.arange(dest_device.shape[0], dtype=jnp.int32)
    same = (dest_device[:, None] == dest_device[None, :]) & (row_ids[:, None] < row_ids[None, :])
    return jnp.sum(same.astype(jnp.int32), axis=0)


def live_mask(lengths_block, row_total):
    row_ids = jnp.arange(row_total, dtype=jnp.int32)
    utterance = row_ids // LMAX
    frame_pos = row_ids % LMAX
    picks = utterance[None, :] == jnp.arange(lengths_block.shape[0], dtype=jnp.int32)[:, None]
    row_length = jnp.sum(jnp.where(picks, lengths_block[:, None], 0), axis=0)
    return (frame_pos < row_length).astype(F32)


def shape(*dims, dtype=F32):
    return jax.ShapeDtypeStruct(dims, dtype)


def call(kernel, scalars, arrays, out_shape, grant, scratch=()):
    in_specs = [pl.BlockSpec(memory_space=pltpu.SMEM)] if scalars is not None else []
    operands = [scalars] if scalars is not None else []
    out_specs = jax.tree.map(lambda _: pl.BlockSpec(memory_space=pltpu.VMEM), out_shape)
    return pl.pallas_call(
        kernel,
        in_specs=in_specs + [pl.BlockSpec(memory_space=pltpu.VMEM) for _ in arrays],
        out_specs=out_specs,
        out_shape=out_shape,
        scratch_shapes=list(scratch),
        compiler_params=pltpu.CompilerParams(vmem_limit_bytes=grant << 20),
    )(*operands, *arrays)


def on_core(core, cores, run):
    for index in range(cores):
        pl.when(core == index)(functools.partial(run, index))


def soft_kernel(half, cores, ids_ref, logits_ref, weight_ref, hot_ref, target_ref, mine_ref, other_ref, mass_ref, powers_ref):
    vocab, rows = logits_ref.shape
    block = math.gcd(half, vocab - half)

    def rows_at(index):
        return pl.ds(pl.multiple_of(index * block, block), block)

    def highest(index, top):
        values = logits_ref[rows_at(index), :].astype(F32)
        return jnp.maximum(top, jnp.max(values, axis=0, keepdims=True))

    top = lax.fori_loop(
        0, vocab // block, highest, jnp.full((1, rows), -jnp.inf, F32), unroll=5
    )

    def raised(index, total):
        powers = jnp.exp(logits_ref[rows_at(index), :].astype(F32) - top)
        powers_ref[rows_at(index), :] = powers
        return total + jnp.sum(powers, axis=0, keepdims=True)

    total = lax.fori_loop(0, vocab // block, raised, jnp.zeros((1, rows), F32), unroll=5)
    scale = weight_ref[...] / total
    hot = hot_ref[...]
    places = lax.broadcasted_iota(jnp.int32, (block, rows), 0)

    def write(out_ref, start, count, mass):
        def one(index, mass):
            at = index * block + start
            soft = powers_ref[pl.ds(pl.multiple_of(at, block), block), :] * scale
            soft = soft + jnp.where(places + at == target_ref[...], hot, 0.0)
            soft = soft.astype(BF16)
            out_ref[rows_at(index), :] = soft
            return mass + jnp.sum(soft.astype(F32), axis=0, keepdims=True)

        return lax.fori_loop(0, count // block, one, mass, unroll=4)

    def run(core):
        refs = (mine_ref, other_ref)
        low_ref, high_ref = refs if core == 0 else refs[::-1]
        mass = write(low_ref, 0, half, jnp.zeros((1, rows), F32))
        mass_ref[...] = write(high_ref, half, vocab - half, mass)
        high_ref[vocab - half :, :] = jnp.zeros((2 * half - vocab, rows), BF16)

    on_core(ids_ref[0], cores, run)


def select_kernel(
    cores, chips, plans, ids_ref, place_ref, near_ref, far_ref, gain_ref,
    normed_ref, scaled_ref, *refs,
):
    state_refs, turned_ref = refs[:-1], refs[-1]
    rows = place_ref.shape[1]
    count = near_ref.shape[0]
    width = near_ref.shape[1]
    block = width // (cores * chips)
    ids = lax.broadcasted_iota(jnp.int32, (count, rows), 0)
    place = place_ref[...]

    def taken(hit, states_ref):
        return lax.dot_general(
            hit.astype(F32).astype(BF16),
            states_ref[...],
            CONTRACT_FIRST,
            preferred_element_type=F32,
        )

    hidden = taken(place == ids, near_ref) + taken(place - count == ids, far_ref)
    centre = jnp.mean(hidden, axis=1, keepdims=True)
    moved = hidden - centre
    spread = jnp.mean(moved * moved, axis=1, keepdims=True)
    normed = moved * lax.rsqrt(spread + EPSILON)
    normed_ref[...] = normed
    scaled = normed * gain_ref[...]
    scaled_ref[...] = scaled.astype(BF16)
    turned_ref[...] = scaled.T
    refs = iter(state_refs)
    for side, ((stride, size), strides) in enumerate(plans):
        for step in range(size):
            to_near = lax.rem(ids_ref[1 + side] + step, size) * stride
            places = [0]
            for far in strides:
                places = [at + bit * far for at in places for bit in (0, 1)]
            groups = []
            for at in places:
                for core in range(cores):
                    first = (core * chips + at + to_near) * block
                    groups.append(turned_ref[pl.ds(pl.multiple_of(first, block), block), :])
            next(refs)[...] = jnp.concatenate(groups, axis=0).astype(BF16)


def forward_kernel(
    cores, tile, ids_ref, scaled_ref, weight_ref, bias_ref, mine_ref, other_ref,
    powers_ref, stats_ref, dots_ref,
):
    vocab = weight_ref.shape[0]
    rows = scaled_ref.shape[0]

    def run(core):
        scaled = scaled_ref[...]
        dots = jnp.zeros((1, rows), F32)
        for index in range(TILES):
            first = (core * TILES + index) * tile
            count = max(0, min(tile, vocab - first))
            at = slice(index * tile, index * tile + count)
            logits = lax.dot_general(
                weight_ref[first : first + count, :], scaled, CONTRACT_LAST,
                preferred_element_type=F32,
            )
            bias = jnp.broadcast_to(bias_ref[:, first : first + count], (LANES, count)).T
            logits = logits + jnp.concatenate([bias] * (rows // LANES), axis=1)
            top = jnp.max(logits, axis=0, keepdims=True)
            powers = jnp.exp(logits - top)
            powers_ref[at, :] = powers
            if count < tile:
                powers_ref[index * tile + count : (index + 1) * tile, :] = jnp.zeros(
                    (tile - count, rows), F32
                )
            soft = mine_ref[at, :].astype(F32) + other_ref[at, :].astype(F32)
            stats_ref[index : index + 1, :] = top
            stats_ref[TILES + index : TILES + index + 1, :] = jnp.sum(
                powers, axis=0, keepdims=True
            )
            dots = dots + jnp.sum(soft * logits, axis=0, keepdims=True)
        dots_ref[...] = dots

    on_core(ids_ref[0], cores, run)


def grad_kernel(
    turn, powers_ref, stats_ref, stats_far_ref, mass_ref, mass_far_ref, dots_ref,
    mine_ref, other_ref, first_ref, second_ref, loss_ref,
):
    stats, stats_far = stats_ref[...], stats_far_ref[...]
    tops, tops_far = stats[:TILES], stats_far[:TILES]
    top = jnp.maximum(
        jnp.max(tops, axis=0, keepdims=True), jnp.max(tops_far, axis=0, keepdims=True)
    )
    shrunk = jnp.exp(tops - top)
    terms = stats[TILES:] * shrunk + stats_far[TILES:] * jnp.exp(tops_far - top)
    total = jnp.sum(terms, axis=0, keepdims=True)
    mass = mass_ref[...] + mass_far_ref[...]
    scale = shrunk * (mass / total)
    tile = first_ref.shape[0]
    for index, out_ref in ((turn, first_ref), (turn + TURNS, second_ref)):
        at = slice(index * tile, (index + 1) * tile)
        grad = powers_ref[at, :] * scale[index : index + 1]
        grad = grad - mine_ref[at, :].astype(F32) - other_ref[at, :].astype(F32)
        out_ref[...] = grad.astype(BF16)
    loss = 0.5 * mass * (top + jnp.log(total)) - dots_ref[...]
    loss_ref[...] = jnp.broadcast_to(jnp.sum(loss, axis=1, keepdims=True), loss_ref.shape)


def back_kernel(cores, tile, ids_ref, weight_ref, normed_ref, loss_ref, live_ref, *refs):
    grads, out_ref = refs[:TILES], refs[TILES]
    vocab, width = weight_ref.shape
    rows = normed_ref.shape[0]
    half = TILES * tile
    ones = jnp.ones((8, rows), BF16)

    def run(core):
        total = None
        for index in range(TILES):
            first = (core * TILES + index) * tile
            count = max(0, min(tile, vocab - first))
            grad = grads[index][...]
            sums = lax.dot_general(ones, grad, CONTRACT_LAST, preferred_element_type=F32)
            out_ref[:, index * tile : (index + 1) * tile] = sums[:1]
            term = lax.dot_general(
                grads[index][:count, :], weight_ref[first : first + count, :], CONTRACT_FIRST,
                preferred_element_type=F32,
            )
            total = term if total is None else total + term
        out_ref[:, half : half + width] = jnp.sum(total * normed_ref[...], axis=0, keepdims=True)

    on_core(ids_ref[0], cores, run)
    lane = lax.broadcasted_iota(jnp.int32, (1, LANES), 1)
    frames = jnp.sum(live_ref[...], axis=1, keepdims=True)
    out_ref[:, half + width :] = jnp.where(
        lane == 0, loss_ref[...], jnp.where(lane == 1, frames, 0.0)
    )


def term_kernel(near, ids_ref, *refs):
    states, grads, (kept_ref, sent_ref) = refs[:near], refs[near : 2 * near], refs[2 * near :]
    count = kept_ref.shape[0]

    def product(side):
        rows = pl.ds(pl.multiple_of(side * count, count), count)
        total = None
        for state, grad in zip(states, grads):
            term = lax.dot_general(
                state[rows, :], grad[...], CONTRACT_LAST, preferred_element_type=F32
            )
            total = term if total is None else total + term
        return total

    sent_ref[...] = product(1 - ids_ref[0]).astype(BF16)
    kept_ref[...] = product(ids_ref[0])


def halve_kernel(parts, ids_ref, *refs):
    kept, came, (kept_ref, sent_ref) = refs[:parts], refs[parts : 2 * parts], refs[2 * parts :]
    count, width = kept_ref.shape
    width = width // parts
    for index in range(parts):
        at = slice(index * width, (index + 1) * width)

        def total(side):
            rows = pl.ds(pl.multiple_of(side * count, count), count)
            return kept[index][rows, :] + came[index][rows, :].astype(F32)

        sent_ref[:, at] = total(1 - ids_ref[0]).astype(BF16)
        kept_ref[:, at] = total(ids_ref[0])


def halve(bit, kept, came):
    count = kept[0].shape[0] // 2
    width = sum(part.shape[1] for part in kept)
    return call(
        functools.partial(halve_kernel, len(kept)),
        bit[None],
        [*kept, *came],
        [shape(count, width), shape(count, width, dtype=BF16)],
        6,
    )


def split_kernel(tile, ids_ref, *refs):
    kept, came, (mine_ref, sent_ref) = refs[:TURNS], refs[TURNS : 2 * TURNS], refs[2 * TURNS :]
    count = mine_ref.shape[0]

    def total(turn, core):
        rows = pl.ds(pl.multiple_of(core * count, count), count)
        return kept[turn][rows, :] + came[turn][rows, :].astype(F32)

    for turn in range(TURNS):
        for out_ref, core in ((mine_ref, ids_ref[0]), (sent_ref, 1 - ids_ref[0])):
            both = total(turn, core)
            out_ref[:, turn * tile : (turn + 1) * tile] = both[:, :tile]
            far = (turn + TURNS) * tile
            out_ref[:, far : far + tile] = both[:, tile:]


def sum_kernel(*refs):
    total = refs[0][...]
    for ref in refs[1:-1]:
        total = total + ref[...]
    refs[-1][...] = total


def small_kernel(cores, half, width, ids_ref, near_ref, far_ref, gain_ref, bias_ref, tail_ref):
    vocab = bias_ref.shape[1]
    tail, tail_far = near_ref[:, half + width :], far_ref[:, half + width :]
    inverse = 1.0 / tail[:, 1:2]
    near, far = near_ref[:, half : half + width], far_ref[:, half : half + width]
    gain_ref[...] = (near + far) * inverse
    lane = lax.broadcasted_iota(jnp.int32, tail.shape, 1)
    tail_ref[...] = jnp.where(lane == 0, (tail + tail_far) * inverse, inverse)

    def run(core):
        low, high = (near_ref, far_ref) if core == 0 else (far_ref, near_ref)
        bias_ref[:, :half] = low[:, :half] * inverse
        bias_ref[:, half:] = high[:, : vocab - half] * inverse

    on_core(ids_ref[0], cores, run)


def finish_kernel(cores, ids_ref, mine_ref, came_ref, tail_ref, out_ref):
    half = mine_ref.shape[1]
    vocab = out_ref.shape[1]
    inverse = tail_ref[:, 1:2]

    def run(core):
        low, high = (mine_ref, came_ref) if core == 0 else (came_ref, mine_ref)
        out_ref[:, :half] = low[...] * inverse
        out_ref[:, half:] = high[:, : vocab - half] * inverse

    on_core(ids_ref[0], cores, run)


def body(
    teacher_logits, routes, agreement, targets, lengths, student_hidden, out_weight, out_bias, gain
):
    cores = lax.axis_size("teach")
    chips = lax.axis_size("dp")
    devices = cores * chips
    rows = teacher_logits.shape[1]
    slots = cores * rows // devices
    vocab = teacher_logits.shape[2]
    width = student_hidden.shape[1]
    out_rows = width // devices
    size_a, size_b, size_c = torus_factors(chips)
    bits_a, bits_b, bits_c = bits_of(size_a), bits_of(size_b), bits_of(size_c)
    tile = -(-vocab // (TILES * cores * LANES)) * LANES
    half = TILES * tile
    core = lax.axis_index("teach").astype(jnp.int32)
    chip = lax.axis_index("dp").astype(jnp.int32)
    ids = core[None]
    exchange = [(i, 1 - i) for i in range(cores)]
    deep = [size_a * size_b << k for k in range(bits_c)]
    plans = (
        ((1, size_a), [size_a << k for k in range(bits_b)] + deep),
        ((size_a, size_b), [1 << k for k in range(bits_a)] + deep),
    )

    def swap(value):
        return lax.ppermute(value, "teach", exchange)

    def bit_of(stride):
        return (chip // stride) % 2

    def along(value, stride, size, step):
        return lax.ppermute(value, "dp", rotation(chips, stride, size, step))

    def flip(value, mask):
        return lax.ppermute(value, "dp", [(i, i ^ mask) for i in range(chips)])

    arrived = lax.all_to_all(
        student_hidden.reshape(chips, slots, width),
        "dp",
        split_axis=0,
        concat_axis=0,
        tiled=True,
    ).reshape(chips * slots, width)
    arrived_far = swap(arrived)

    dest_device = routes[:, 0]
    live_rows = live_mask(lengths, rows)
    mine, other, mass = call(
        functools.partial(soft_kernel, half, cores),
        ids,
        [
            teacher_logits[0].T,
            (0.5 * agreement.astype(F32) * live_rows)[None, :],
            (0.5 * live_rows)[None, :],
            targets[None, :],
        ],
        [shape(half, rows, dtype=BF16), shape(half, rows, dtype=BF16), shape(1, rows)],
        8,
        [pltpu.VMEM((vocab, rows), F32)],
    )
    other = swap(other)
    mass_far = swap(mass)

    place = (dest_device % chips) * slots + route_slots(dest_device)
    place = jnp.where(dest_device // chips == core, place, place + chips * slots)
    near_ids = [(chip // stride) % size for (stride, size), _ in plans]
    normed, scaled, *own_states = call(
        functools.partial(select_kernel, cores, chips, plans),
        jnp.stack([core, *near_ids]),
        [place[None, :], arrived, arrived_far, gain[None, :]],
        [shape(rows, width), shape(rows, width, dtype=BF16)]
        + [shape(width // size, rows, dtype=BF16) for (_, size), _ in plans for _ in range(size)],
        12,
        [pltpu.VMEM((width, rows), F32)],
    )
    states = []
    for (stride, size), _ in plans:
        states.append(
            [
                along(piece, stride, size, step) if step else piece
                for step, piece in enumerate(own_states[:size])
            ]
        )
        own_states = own_states[size:]

    weight = out_weight.T
    powers, stats, dots = call(
        functools.partial(forward_kernel, cores, tile),
        ids,
        [scaled, weight, out_bias[None, :], mine, other],
        [shape(half, rows), shape(2 * TILES, rows), shape(1, rows)],
        12,
    )
    stats_far = swap(stats)

    grads = [None] * TILES
    for turn in range(TURNS):
        grads[turn], grads[turn + TURNS], loss = call(
            functools.partial(grad_kernel, turn),
            None,
            [powers, stats, stats_far, mass, mass_far, dots, mine, other],
            [shape(tile, rows, dtype=BF16)] * 2 + [shape(1, LANES)],
            6,
        )

    gathered = {}
    for turn in range(TURNS):
        for side, ((stride, size), _) in enumerate(plans):
            grad = grads[turn + TURNS * side]
            gathered[turn, side] = [
                along(grad, stride, size, step) if step else grad for step in range(size)
            ]

    ends = []
    for turn in range(TURNS):
        kept, came = [], []
        for side, ((_, size), strides) in enumerate(plans):
            count = width // size // 2
            part, sent = call(
                functools.partial(term_kernel, size),
                bit_of(strides[0])[None],
                [*states[side], *gathered[turn, side]],
                [shape(count, tile), shape(count, tile, dtype=BF16)],
                6,
            )
            for depth, stride in enumerate(strides[: len(strides) - bits_c]):
                if depth:
                    part, sent = halve(bit_of(stride), [part], [got])
                got = flip(sent, stride)
            kept.append(part)
            came.append(got)
        for stride in deep:
            part, sent = halve(bit_of(stride), kept, came)
            kept, came = [part], [flip(sent, stride)]
        ends += kept + came

    small = call(
        functools.partial(back_kernel, cores, tile),
        ids,
        [weight, normed, loss, live_rows[None, :], *grads],
        shape(1, half + width + LANES),
        10,
    )
    for strides in (deep, [1 << k for k in range(bits_a + bits_b)]):
        got = [flip(small, mask) for mask in flips(strides)]
        small = call(sum_kernel, None, [small, *got], shape(*small.shape), 2)
    small_far = swap(small)
    gain_sum, bias_sum, tail = call(
        functools.partial(small_kernel, cores, half, width),
        ids,
        [small, small_far],
        [shape(1, width), shape(1, vocab), shape(1, LANES)],
        2,
    )

    own, sent = call(
        functools.partial(split_kernel, tile),
        ids,
        ends[::2] + ends[1::2],
        [shape(out_rows, half)] * 2,
        4,
    )
    weight_grad = call(
        functools.partial(finish_kernel, cores),
        ids,
        [own, swap(sent), tail],
        shape(out_rows, vocab),
        4,
    )
    return (weight_grad, gain_sum[0], bias_sum[0], tail[0, 0])


def solution(mesh):
    return jax.shard_map(
        body,
        mesh=mesh,
        in_specs=(
            P("teach", "dp", None),
            P("dp", None),
            P("dp"),
            P("dp"),
            P("dp"),
            P(("teach", "dp"), None),
            P(),
            P(),
            P(),
        ),
        out_specs=(P(("teach", "dp"), None), P(), P(), P()),
        check_vma=False,
    )
```

```python
import functools
import math

import jax
import jax.numpy as jnp
from jax import lax
from jax.experimental import pallas as pl
from jax.experimental.pallas import tpu as pltpu
from jax.sharding import PartitionSpec as P


LMAX = 256
EPSILON = 1e-05
LANES = 128
TURNS = 2
TILES = 2 * TURNS
F32 = jnp.float32
BF16 = jnp.bfloat16
CONTRACT_LAST = (((1,), (1,)), ((), ()))
CONTRACT_FIRST = (((0,), (0,)), ((), ()))


def bits_of(count):
    return count.bit_length() - 1


def torus_factors(count):
    bits = bits_of(count)
    small = bits // 3
    middle = (bits - small) // 2
    return 1 << small, 1 << middle, 1 << (bits - small - middle)


def rotation(count, stride, size, step):
    def moved(index):
        place = (index // stride) % size
        return index + ((place + step) % size - place) * stride

    return [(index, moved(index)) for index in range(count)]


def tile_plan(vocab, cores):
    groups = -(-vocab // (2 * cores * LANES))
    sizes = [(groups + turn) // TURNS * LANES for turn in range(TURNS)]
    starts = [0]
    for size in sizes * 2:
        starts.append(starts[-1] + size)
    return sizes * 2, starts[:-1], starts[-1]


def route_slots(dest_device):
    row_ids = jnp.arange(dest_device.shape[0], dtype=jnp.int32)
    same = (dest_device[:, None] == dest_device[None, :]) & (row_ids[:, None] < row_ids[None, :])
    return jnp.sum(same.astype(jnp.int32), axis=0)


def live_mask(lengths_block, row_total):
    row_ids = jnp.arange(row_total, dtype=jnp.int32)
    utterance = row_ids // LMAX
    frame_pos = row_ids % LMAX
    picks = utterance[None, :] == jnp.arange(lengths_block.shape[0], dtype=jnp.int32)[:, None]
    row_length = jnp.sum(jnp.where(picks, lengths_block[:, None], 0), axis=0)
    return (frame_pos < row_length).astype(F32)


def shape(*dims, dtype=F32):
    return jax.ShapeDtypeStruct(dims, dtype)


class Pulled:
    def __init__(self, value):
        self.value = value


def call(kernel, scalars, arrays, out_shape, grant, scratch=(), fetched=0):
    operands, in_specs, pulled = [], [], []
    if scalars is not None:
        operands.append(scalars)
        in_specs.append(pl.BlockSpec(memory_space=pltpu.SMEM))
    lead = len(operands)
    for index, array in enumerate(arrays):
        space = pltpu.VMEM
        if isinstance(array, Pulled):
            array, space = array.value, pl.ANY
            pulled.append(lead + index)
        elif index < fetched:
            space = pltpu.HBM
        operands.append(array)
        in_specs.append(pl.BlockSpec(memory_space=space))
    buffers = [pltpu.VMEM(operands[index].shape, operands[index].dtype) for index in pulled]
    if pulled:
        buffers.append(pltpu.SemaphoreType.DMA((len(pulled),)))

    def run(*refs):
        refs = list(refs)
        if pulled:
            held, arrived = refs[-len(buffers) : -1], refs[-1]
            refs = refs[: -len(buffers)]
            copies = [
                pltpu.make_async_copy(refs[index], buffer, arrived.at[place])
                for place, (index, buffer) in enumerate(zip(pulled, held))
            ]
            for copy in copies:
                copy.start()
            for copy in copies:
                copy.wait()
            for index, buffer in zip(pulled, held):
                refs[index] = buffer
        kernel(*refs)

    return pl.pallas_call(
        run,
        in_specs=in_specs,
        out_specs=jax.tree.map(lambda _: pl.BlockSpec(memory_space=pltpu.VMEM), out_shape),
        out_shape=out_shape,
        scratch_shapes=list(scratch) + buffers,
        compiler_params=pltpu.CompilerParams(vmem_limit_bytes=grant << 20),
    )(*operands)


def in_hbm(value):
    return pltpu.with_memory_space_constraint(value, pltpu.HBM)


def on_core(core, cores, run):
    for index in range(cores):
        pl.when(core == index)(functools.partial(run, index))


def soft_kernel(half, cores, ids_ref, logits_ref, weight_ref, hot_ref, target_ref, mine_ref, other_ref, mass_ref, powers_ref):
    vocab, rows = logits_ref.shape
    block = math.gcd(half, vocab - half)

    def rows_at(index):
        return pl.ds(pl.multiple_of(index * block, block), block)

    def highest(index, top):
        values = logits_ref[rows_at(index), :].astype(F32)
        return jnp.maximum(top, jnp.max(values, axis=0, keepdims=True))

    top = lax.fori_loop(
        0, vocab // block, highest, jnp.full((1, rows), -jnp.inf, F32), unroll=5
    )

    def raised(index, total):
        powers = jnp.exp(logits_ref[rows_at(index), :].astype(F32) - top)
        powers_ref[rows_at(index), :] = powers
        return total + jnp.sum(powers, axis=0, keepdims=True)

    total = lax.fori_loop(0, vocab // block, raised, jnp.zeros((1, rows), F32), unroll=5)
    scale = weight_ref[...] / total
    hot = hot_ref[...]
    places = lax.broadcasted_iota(jnp.int32, (block, rows), 0)

    def write(out_ref, start, count, mass):
        def one(index, mass):
            at = index * block + start
            soft = powers_ref[pl.ds(pl.multiple_of(at, block), block), :] * scale
            soft = soft + jnp.where(places + at == target_ref[...], hot, 0.0)
            soft = soft.astype(BF16)
            out_ref[rows_at(index), :] = soft
            return mass + jnp.sum(soft.astype(F32), axis=0, keepdims=True)

        return lax.fori_loop(0, count // block, one, mass, unroll=4)

    def run(core):
        refs = (mine_ref, other_ref)
        low_ref, high_ref = refs if core == 0 else refs[::-1]
        mass = write(low_ref, 0, half, jnp.zeros((1, rows), F32))
        mass_ref[...] = write(high_ref, half, vocab - half, mass)
        high_ref[vocab - half :, :] = jnp.zeros((2 * half - vocab, rows), BF16)

    on_core(ids_ref[0], cores, run)


def weight_copies(core, vocab, sizes, starts, half, weight_ref, held_ref, arrived):
    tiles = []
    for index, (size, start) in enumerate(zip(sizes, starts)):
        first = core * half + start
        count = max(0, min(size, vocab - first))
        copy = pltpu.make_async_copy(
            weight_ref.at[pl.ds(first, count), :],
            held_ref.at[pl.ds(start, count), :],
            arrived.at[index],
        )
        tiles.append((count, copy))
    return tiles


def student_kernel(
    cores, chips, plans, tiling, ids_ref, weight_ref, place_ref, near_ref, far_ref, gain_ref,
    bias_ref, mine_ref, other_ref, normed_ref, powers_ref, stats_ref, dots_ref, *refs,
):
    state_refs, (turned_ref, held_ref, arrived) = refs[:-3], refs[-3:]
    rows = place_ref.shape[1]
    count = near_ref.shape[0]
    vocab, width = weight_ref.shape
    block = width // (cores * chips)
    sizes, starts, half = tiling

    def copies(core):
        return weight_copies(core, vocab, sizes, starts, half, weight_ref, held_ref, arrived)

    def fetch(core):
        for _, copy in copies(core):
            copy.start()

    on_core(ids_ref[0], cores, fetch)
    ids = lax.broadcasted_iota(jnp.int32, (count, rows), 0)
    place = place_ref[...]

    def taken(hit, states_ref):
        return lax.dot_general(
            hit.astype(F32).astype(BF16),
            states_ref[...],
            CONTRACT_FIRST,
            preferred_element_type=F32,
        )

    hidden = taken(place == ids, near_ref) + taken(place - count == ids, far_ref)
    centre = jnp.mean(hidden, axis=1, keepdims=True)
    moved = hidden - centre
    spread = jnp.mean(moved * moved, axis=1, keepdims=True)
    normed = moved * lax.rsqrt(spread + EPSILON)
    normed_ref[...] = normed
    scaled = normed * gain_ref[...]
    turned_ref[...] = scaled.T
    scaled = scaled.astype(BF16)
    refs = iter(state_refs)
    for side, ((stride, size), strides) in enumerate(plans):
        for step in range(size):
            to_near = lax.rem(ids_ref[1 + side] + step, size) * stride
            places = [0]
            for far in strides[1:] if step else strides:
                places = [at + bit * far for at in places for bit in (0, 1)]
            if step:
                to_near = to_near + ids_ref[0] * strides[0]
            groups = []
            for at in places:
                for core in range(cores):
                    first = (core * chips + at + to_near) * block
                    groups.append(turned_ref[pl.ds(pl.multiple_of(first, block), block), :])
            next(refs)[...] = jnp.concatenate(groups, axis=0).astype(BF16)

    def run(core):
        dots = jnp.zeros((1, rows), F32)
        tiles = copies(core)
        for _, copy in tiles:
            copy.wait()
        for index, (count, _) in enumerate(tiles):
            first = core * half + starts[index]
            at = slice(starts[index], starts[index] + count)
            logits = lax.dot_general(
                held_ref[at, :], scaled, CONTRACT_LAST, preferred_element_type=F32
            )
            bias = jnp.broadcast_to(bias_ref[:, first : first + count], (LANES, count)).T
            logits = logits + jnp.concatenate([bias] * (rows // LANES), axis=1)
            top = jnp.max(logits, axis=0, keepdims=True)
            powers = jnp.exp(logits - top)
            powers_ref[at, :] = powers
            if count < sizes[index]:
                powers_ref[starts[index] + count : starts[index] + sizes[index], :] = jnp.zeros(
                    (sizes[index] - count, rows), F32
                )
            soft = mine_ref[at, :].astype(F32) + other_ref[at, :].astype(F32)
            stats_ref[index : index + 1, :] = top
            stats_ref[TILES + index : TILES + index + 1, :] = jnp.sum(
                powers, axis=0, keepdims=True
            )
            dots = dots + jnp.sum(soft * logits, axis=0, keepdims=True)
        dots_ref[...] = dots

    on_core(ids_ref[0], cores, run)


def grad_kernel(
    turn, starts, powers_ref, stats_ref, stats_far_ref, mass_ref, mass_far_ref, dots_ref,
    mine_ref, other_ref, first_ref, second_ref, loss_ref,
):
    stats, stats_far = stats_ref[...], stats_far_ref[...]
    tops, tops_far = stats[:TILES], stats_far[:TILES]
    top = jnp.maximum(
        jnp.max(tops, axis=0, keepdims=True), jnp.max(tops_far, axis=0, keepdims=True)
    )
    shrunk = jnp.exp(tops - top)
    terms = stats[TILES:] * shrunk + stats_far[TILES:] * jnp.exp(tops_far - top)
    total = jnp.sum(terms, axis=0, keepdims=True)
    mass = mass_ref[...] + mass_far_ref[...]
    scale = shrunk * (mass / total)
    for index, out_ref in ((turn, first_ref), (turn + TURNS, second_ref)):
        at = slice(starts[index], starts[index] + out_ref.shape[0])
        grad = powers_ref[at, :] * scale[index : index + 1]
        grad = grad - mine_ref[at, :].astype(F32) - other_ref[at, :].astype(F32)
        out_ref[...] = grad.astype(BF16)
    loss = 0.5 * mass * (top + jnp.log(total)) - dots_ref[...]
    loss_ref[...] = jnp.broadcast_to(jnp.sum(loss, axis=1, keepdims=True), loss_ref.shape)


def back_kernel(
    cores, tiling, ids_ref, weight_ref, normed_ref, loss_ref, live_ref, *refs
):
    grads, (out_ref, held_ref, arrived) = refs[:TILES], refs[TILES:]
    vocab, width = weight_ref.shape
    rows = normed_ref.shape[0]
    sizes, starts, half = tiling
    ones = jnp.ones((8, rows), BF16)

    def run(core):
        tiles = weight_copies(core, vocab, sizes, starts, half, weight_ref, held_ref, arrived)
        for _, copy in tiles:
            copy.start()
        for grad_ref, start, size in zip(grads, starts, sizes):
            sums = lax.dot_general(ones, grad_ref[...], CONTRACT_LAST, preferred_element_type=F32)
            out_ref[:, start : start + size] = sums[:1]
        total = None
        for grad_ref, start, (count, copy) in zip(grads, starts, tiles):
            copy.wait()
            term = lax.dot_general(
                grad_ref[:count, :], held_ref[start : start + count, :], CONTRACT_FIRST,
                preferred_element_type=F32,
            )
            total = term if total is None else total + term
        out_ref[:, half : half + width] = jnp.sum(total * normed_ref[...], axis=0, keepdims=True)

    on_core(ids_ref[0], cores, run)
    lane = lax.broadcasted_iota(jnp.int32, (1, LANES), 1)
    frames = jnp.sum(live_ref[...], axis=1, keepdims=True)
    out_ref[:, half + width :] = jnp.where(
        lane == 0, loss_ref[...], jnp.where(lane == 1, frames, 0.0)
    )


def term_kernel(near, ids_ref, own_ref, *refs):
    came, grads = refs[: 2 * (near - 1)], refs[2 * (near - 1) : 3 * near - 2]
    kept_ref, sent_ref, *halves = refs[3 * near - 2 :]
    count = kept_ref.shape[0]
    for index, half_ref in enumerate(halves):
        half_ref[ids_ref[1]] = came[2 * index][...]
        half_ref[1 - ids_ref[1]] = came[2 * index + 1][...]

    def product(side):
        rows = pl.ds(pl.multiple_of(side * count, count), count)
        total = None
        for state, grad in zip(
            [own_ref[rows, :]] + [half_ref[side] for half_ref in halves], grads
        ):
            term = lax.dot_general(state, grad[...], CONTRACT_LAST, preferred_element_type=F32)
            total = term if total is None else total + term
        return total

    sent_ref[...] = product(1 - ids_ref[0]).astype(BF16)
    kept_ref[...] = product(ids_ref[0])


def halve_kernel(parts, ids_ref, *refs):
    came, kept = refs[:parts], refs[parts : 2 * parts]
    kept_ref, sent_ref = refs[2 * parts :]
    count, width = kept_ref.shape
    width = width // parts
    for index in range(parts):
        at = slice(index * width, (index + 1) * width)

        def total(side):
            rows = pl.ds(pl.multiple_of(side * count, count), count)
            return kept[index][rows, :] + came[index][rows, :].astype(F32)

        sent_ref[:, at] = total(1 - ids_ref[0]).astype(BF16)
        kept_ref[:, at] = total(ids_ref[0])


def halve(bit, kept, came):
    count = kept[0].shape[0] // 2
    width = sum(part.shape[1] for part in kept)
    kept, sent = call(
        functools.partial(halve_kernel, len(kept)),
        bit[None],
        [*map(Pulled, came), *map(Pulled, kept)],
        [shape(count, width), shape(count, width, dtype=BF16)],
        8,
    )
    return kept, sent


def split_kernel(tiling, ids_ref, *refs):
    kept, came, (mine_ref, sent_ref) = refs[:TURNS], refs[TURNS : 2 * TURNS], refs[2 * TURNS :]
    count = mine_ref.shape[0]
    sizes, starts, _ = tiling

    def total(turn, core):
        rows = pl.ds(pl.multiple_of(core * count, count), count)
        return kept[turn][rows, :] + came[turn][rows, :].astype(F32)

    for turn in range(TURNS):
        size = sizes[turn]
        for out_ref, core in ((mine_ref, ids_ref[0]), (sent_ref, 1 - ids_ref[0])):
            both = total(turn, core)
            out_ref[:, starts[turn] : starts[turn] + size] = both[:, :size]
            far = starts[turn + TURNS]
            out_ref[:, far : far + size] = both[:, size:]


def sum_kernel(*refs):
    total = refs[0][...]
    for ref in refs[1:-1]:
        total = total + ref[...]
    refs[-1][...] = total


def small_kernel(
    cores, half, width, ids_ref, near_ref, far_ref, gain_ref, bias_ref, loss_ref, scale_ref
):
    vocab = bias_ref.shape[1]
    tail, tail_far = near_ref[:, half + width :], far_ref[:, half + width :]
    inverse = 1.0 / tail[:, 1:2]
    near, far = near_ref[:, half : half + width], far_ref[:, half : half + width]
    gain_ref[...] = (near + far) * inverse
    loss_ref[...] = (tail + tail_far) * inverse
    scale_ref[...] = jnp.broadcast_to(inverse, scale_ref.shape)

    def run(core):
        low, high = (near_ref, far_ref) if core == 0 else (far_ref, near_ref)
        bias_ref[:, :half] = low[:, :half] * inverse
        bias_ref[:, half:] = high[:, : vocab - half] * inverse

    on_core(ids_ref[0], cores, run)


def finish_kernel(cores, ids_ref, mine_ref, came_ref, scale_ref, out_ref):
    half = mine_ref.shape[1]
    vocab = out_ref.shape[1]
    inverse = scale_ref[:, :1]

    def run(core):
        low, high = (mine_ref, came_ref) if core == 0 else (came_ref, mine_ref)
        out_ref[:, :half] = low[...] * inverse
        out_ref[:, half:] = high[:, : vocab - half] * inverse

    on_core(ids_ref[0], cores, run)


def body(
    teacher_logits, routes, agreement, targets, lengths, student_hidden, out_weight, out_bias, gain
):
    cores = lax.axis_size("teach")
    chips = lax.axis_size("dp")
    devices = cores * chips
    rows = teacher_logits.shape[1]
    slots = cores * rows // devices
    vocab = teacher_logits.shape[2]
    width = student_hidden.shape[1]
    out_rows = width // devices
    size_a, size_b, size_c = torus_factors(chips)
    bits_a, bits_b, bits_c = bits_of(size_a), bits_of(size_b), bits_of(size_c)
    tiling = tile_plan(vocab, cores)
    sizes, starts, half = tiling
    core = lax.axis_index("teach").astype(jnp.int32)
    chip = lax.axis_index("dp").astype(jnp.int32)
    ids = core[None]
    exchange = [(i, 1 - i) for i in range(cores)]
    deep = [size_a * size_b << k for k in range(bits_c)]
    plans = (
        ((1, size_a), [size_a << k for k in range(bits_b)] + deep),
        ((size_a, size_b), [1 << k for k in range(bits_a)] + deep),
    )

    def swap(value):
        return lax.ppermute(value, "teach", exchange)

    def bit_of(stride):
        return (chip // stride) % 2

    def along(value, stride, size, step):
        return lax.ppermute(value, "dp", rotation(chips, stride, size, step))

    def flip(value, mask):
        return lax.ppermute(value, "dp", [(i, i ^ mask) for i in range(chips)])

    arrived = lax.all_to_all(
        student_hidden.reshape(chips, slots, width),
        "dp",
        split_axis=0,
        concat_axis=0,
        tiled=True,
    ).reshape(chips * slots, width)
    arrived_far = swap(arrived)

    dest_device = routes[:, 0]
    live_rows = live_mask(lengths, rows)
    mine, other, mass = call(
        functools.partial(soft_kernel, half, cores),
        ids,
        [
            teacher_logits[0].T,
            (0.5 * agreement.astype(F32) * live_rows)[None, :],
            (0.5 * live_rows)[None, :],
            targets[None, :],
        ],
        [shape(half, rows, dtype=BF16), shape(half, rows, dtype=BF16), shape(1, rows)],
        8,
        [pltpu.VMEM((vocab, rows), F32)],
    )
    other = swap(other)
    mass_far = swap(mass)

    place = (dest_device % chips) * slots + route_slots(dest_device)
    place = jnp.where(dest_device // chips == core, place, place + chips * slots)
    near_ids = [(chip // stride) % size for (stride, size), _ in plans]
    weight = in_hbm(out_weight.T)
    held = [pltpu.VMEM((half, width), BF16), pltpu.SemaphoreType.DMA((TILES,))]
    normed, powers, stats, dots, *own_states = call(
        functools.partial(student_kernel, cores, chips, plans, tiling),
        jnp.stack([core, *near_ids]),
        [weight, place[None, :], arrived, arrived_far, gain[None, :], out_bias[None, :], mine, other],
        [shape(rows, width), shape(half, rows), shape(2 * TILES, rows), shape(1, rows)]
        + [
            shape(width // size // (2 if step else 1), rows, dtype=BF16)
            for (_, size), _ in plans
            for step in range(size)
        ],
        24,
        [pltpu.VMEM((width, rows), F32), *held],
        fetched=1,
    )
    stats_far = swap(stats)
    states = []
    for (stride, size), _ in plans:
        group = [own_states[0]]
        for step in range(1, size):
            direct = along(own_states[step], stride, size, step)
            group += [direct, swap(direct)]
        states.append(group)
        own_states = own_states[size:]

    grads = [None] * TILES
    for turn in range(TURNS):
        grads[turn], grads[turn + TURNS], loss = call(
            functools.partial(grad_kernel, turn, starts),
            None,
            [powers, stats, stats_far, mass, mass_far, dots, mine, other],
            [shape(sizes[turn], rows, dtype=BF16)] * 2 + [shape(1, LANES)],
            6,
        )

    gathered = {}
    for turn in range(TURNS):
        for side, ((stride, size), _) in enumerate(plans):
            grad = grads[turn + TURNS * side]
            gathered[turn, side] = [
                along(grad, stride, size, step) if step else grad for step in range(size)
            ]

    ends = []
    for turn in range(TURNS):
        kept, came = [], []
        for side, ((_, size), strides) in enumerate(plans):
            count = width // size // 2
            part, sent = call(
                functools.partial(term_kernel, size),
                jnp.stack([bit_of(strides[0]), core]),
                [*states[side], *gathered[turn, side]],
                [shape(count, sizes[turn]), shape(count, sizes[turn], dtype=BF16)],
                8,
                [pltpu.VMEM((2, count, rows), BF16)] * (size - 1),
            )
            for depth, stride in enumerate(strides[: len(strides) - bits_c]):
                if depth:
                    part, sent = halve(bit_of(stride), [part], [got])
                got = in_hbm(flip(sent, stride))
            kept.append(part)
            came.append(got)
        for stride in deep:
            part, sent = halve(bit_of(stride), kept, came)
            kept, came = [part], [flip(sent, stride)]
        ends += kept + came

    small = call(
        functools.partial(back_kernel, cores, tiling),
        ids,
        [weight, normed, loss, live_rows[None, :], *grads],
        shape(1, half + width + LANES),
        16,
        held,
        fetched=1,
    )
    for stride in deep + [1 << k for k in range(bits_a + bits_b)]:
        got = flip(small, stride)
        small = call(sum_kernel, None, [small, got], shape(*small.shape), 2)
    small_far = swap(small)
    gain_sum, bias_sum, loss_sum, scale = call(
        functools.partial(small_kernel, cores, half, width),
        ids,
        [small, small_far],
        [shape(1, width), shape(1, vocab), shape(1, LANES), shape(1, LANES)],
        2,
    )

    own, sent = call(
        functools.partial(split_kernel, tiling),
        ids,
        [*map(Pulled, ends[::2]), *map(Pulled, ends[1::2])],
        [shape(out_rows, half)] * 2,
        4,
    )
    weight_grad = call(
        functools.partial(finish_kernel, cores),
        ids,
        [Pulled(own), Pulled(swap(sent)), scale],
        shape(out_rows, vocab),
        4,
    )
    return (weight_grad, gain_sum[0], bias_sum[0], loss_sum[0, 0])


def solution(mesh):
    return jax.shard_map(
        body,
        mesh=mesh,
        in_specs=(
            P("teach", "dp", None),
            P("dp", None),
            P("dp"),
            P("dp"),
            P("dp"),
            P(("teach", "dp"), None),
            P(),
            P(),
            P(),
        ),
        out_specs=(P(("teach", "dp"), None), P(), P(), P()),
        check_vma=False,
    )
```

```python
import functools
import math

import jax
import jax.numpy as jnp
from jax import lax
from jax.experimental import pallas as pl
from jax.experimental.pallas import tpu as pltpu
from jax.sharding import PartitionSpec as P


LMAX = 256
EPSILON = 1e-05
LANES = 128
TURNS = 2
TILES = 2 * TURNS
F32 = jnp.float32
BF16 = jnp.bfloat16
CONTRACT_LAST = (((1,), (1,)), ((), ()))
CONTRACT_FIRST = (((0,), (0,)), ((), ()))


def bits_of(count):
    return count.bit_length() - 1


def torus_factors(count):
    bits = bits_of(count)
    small = bits // 3
    middle = (bits - small) // 2
    return 1 << small, 1 << middle, 1 << (bits - small - middle)


def rotation(count, stride, size, step):
    def moved(index):
        place = (index // stride) % size
        return index + ((place + step) % size - place) * stride

    return [(index, moved(index)) for index in range(count)]


def tile_plan(vocab, cores):
    groups = -(-vocab // (2 * cores * LANES))
    sizes = [(groups + turn) // TURNS * LANES for turn in range(TURNS)]
    starts = [0]
    for size in sizes * 2:
        starts.append(starts[-1] + size)
    return sizes * 2, starts[:-1], starts[-1]


def route_slots(dest_device):
    row_ids = jnp.arange(dest_device.shape[0], dtype=jnp.int32)
    same = (dest_device[:, None] == dest_device[None, :]) & (row_ids[:, None] < row_ids[None, :])
    return jnp.sum(same.astype(jnp.int32), axis=0)


def live_mask(lengths_block, row_total):
    row_ids = jnp.arange(row_total, dtype=jnp.int32)
    utterance = row_ids // LMAX
    frame_pos = row_ids % LMAX
    picks = utterance[None, :] == jnp.arange(lengths_block.shape[0], dtype=jnp.int32)[:, None]
    row_length = jnp.sum(jnp.where(picks, lengths_block[:, None], 0), axis=0)
    return (frame_pos < row_length).astype(F32)


def shape(*dims, dtype=F32):
    return jax.ShapeDtypeStruct(dims, dtype)


class Pulled:
    def __init__(self, value):
        self.value = value


def call(kernel, scalars, arrays, out_shape, grant, scratch=(), fetched=0):
    operands, in_specs, pulled = [], [], []
    if scalars is not None:
        operands.append(scalars)
        in_specs.append(pl.BlockSpec(memory_space=pltpu.SMEM))
    lead = len(operands)
    for index, array in enumerate(arrays):
        space = pltpu.VMEM
        if isinstance(array, Pulled):
            array, space = array.value, pl.ANY
            pulled.append(lead + index)
        elif index < fetched:
            space = pltpu.HBM
        operands.append(array)
        in_specs.append(pl.BlockSpec(memory_space=space))
    buffers = [pltpu.VMEM(operands[index].shape, operands[index].dtype) for index in pulled]
    if pulled:
        buffers.append(pltpu.SemaphoreType.DMA((len(pulled),)))

    def run(*refs):
        refs = list(refs)
        if pulled:
            held, arrived = refs[-len(buffers) : -1], refs[-1]
            refs = refs[: -len(buffers)]
            copies = [
                pltpu.make_async_copy(refs[index], buffer, arrived.at[place])
                for place, (index, buffer) in enumerate(zip(pulled, held))
            ]
            for copy in copies:
                copy.start()
            for copy in copies:
                copy.wait()
            for index, buffer in zip(pulled, held):
                refs[index] = buffer
        kernel(*refs)

    return pl.pallas_call(
        run,
        in_specs=in_specs,
        out_specs=jax.tree.map(lambda _: pl.BlockSpec(memory_space=pltpu.VMEM), out_shape),
        out_shape=out_shape,
        scratch_shapes=list(scratch) + buffers,
        compiler_params=pltpu.CompilerParams(vmem_limit_bytes=grant << 20),
    )(*operands)


def in_hbm(value):
    return pltpu.with_memory_space_constraint(value, pltpu.HBM)


def on_core(core, cores, run):
    for index in range(cores):
        pl.when(core == index)(functools.partial(run, index))


def soft_kernel(half, cores, ids_ref, logits_ref, weight_ref, hot_ref, target_ref, mine_ref, other_ref, mass_ref, powers_ref):
    vocab, rows = logits_ref.shape
    block = math.gcd(half, vocab - half)

    def rows_at(index):
        return pl.ds(pl.multiple_of(index * block, block), block)

    def highest(index, top):
        values = logits_ref[rows_at(index), :].astype(F32)
        return jnp.maximum(top, jnp.max(values, axis=0, keepdims=True))

    top = lax.fori_loop(
        0, vocab // block, highest, jnp.full((1, rows), -jnp.inf, F32), unroll=5
    )

    def raised(index, total):
        powers = jnp.exp(logits_ref[rows_at(index), :].astype(F32) - top)
        powers_ref[rows_at(index), :] = powers
        return total + jnp.sum(powers, axis=0, keepdims=True)

    total = lax.fori_loop(0, vocab // block, raised, jnp.zeros((1, rows), F32), unroll=5)
    scale = weight_ref[...] / total
    hot = hot_ref[...]
    places = lax.broadcasted_iota(jnp.int32, (block, rows), 0)

    def write(out_ref, start, count, mass):
        def one(index, mass):
            at = index * block + start
            soft = powers_ref[pl.ds(pl.multiple_of(at, block), block), :] * scale
            soft = soft + jnp.where(places + at == target_ref[...], hot, 0.0)
            soft = soft.astype(BF16)
            out_ref[rows_at(index), :] = soft
            return mass + jnp.sum(soft.astype(F32), axis=0, keepdims=True)

        return lax.fori_loop(0, count // block, one, mass, unroll=4)

    def run(core):
        refs = (mine_ref, other_ref)
        low_ref, high_ref = refs if core == 0 else refs[::-1]
        mass = write(low_ref, 0, half, jnp.zeros((1, rows), F32))
        mass_ref[...] = write(high_ref, half, vocab - half, mass)
        high_ref[vocab - half :, :] = jnp.zeros((2 * half - vocab, rows), BF16)

    on_core(ids_ref[0], cores, run)


def weight_copies(core, vocab, sizes, starts, half, weight_ref, held_ref, arrived):
    tiles = []
    for index, (size, start) in enumerate(zip(sizes, starts)):
        first = core * half + start
        count = max(0, min(size, vocab - first))
        copy = pltpu.make_async_copy(
            weight_ref.at[pl.ds(first, count), :],
            held_ref.at[pl.ds(start, count), :],
            arrived.at[index],
        )
        tiles.append((count, copy))
    return tiles


def student_kernel(
    cores, chips, plans, tiling, ids_ref, weight_ref, place_ref, near_ref, far_ref, gain_ref,
    bias_ref, mine_ref, other_ref, normed_ref, powers_ref, stats_ref, dots_ref, *refs,
):
    state_refs, (turned_ref, held_ref, arrived) = refs[:-3], refs[-3:]
    rows = place_ref.shape[1]
    count = near_ref.shape[0]
    vocab, width = weight_ref.shape
    block = width // (cores * chips)
    sizes, starts, half = tiling

    def copies(core):
        return weight_copies(core, vocab, sizes, starts, half, weight_ref, held_ref, arrived)

    def fetch(tiles, core):
        for _, copy in copies(core)[tiles]:
            copy.start()

    on_core(ids_ref[0], cores, functools.partial(fetch, slice(0, 2)))
    ids = lax.broadcasted_iota(jnp.int32, (count, rows), 0)
    place = place_ref[...]

    def taken(hit, states_ref):
        return lax.dot_general(
            hit.astype(F32).astype(BF16),
            states_ref[...],
            CONTRACT_FIRST,
            preferred_element_type=F32,
        )

    hidden = taken(place == ids, near_ref) + taken(place - count == ids, far_ref)
    on_core(ids_ref[0], cores, functools.partial(fetch, slice(2, None)))
    centre = jnp.mean(hidden, axis=1, keepdims=True)
    moved = hidden - centre
    spread = jnp.mean(moved * moved, axis=1, keepdims=True)
    normed = moved * lax.rsqrt(spread + EPSILON)
    normed_ref[...] = normed
    scaled = normed * gain_ref[...]
    turned_ref[...] = scaled.T
    scaled = scaled.astype(BF16)
    refs = iter(state_refs)
    for side, ((stride, size), strides) in enumerate(plans):
        for step in range(size):
            to_near = lax.rem(ids_ref[1 + side] + step, size) * stride
            places = [0]
            for far in strides[1:] if step else strides:
                places = [at + bit * far for at in places for bit in (0, 1)]
            if step:
                to_near = to_near + ids_ref[0] * strides[0]
            groups = []
            for at in places:
                for core in range(cores):
                    first = (core * chips + at + to_near) * block
                    groups.append(turned_ref[pl.ds(pl.multiple_of(first, block), block), :])
            next(refs)[...] = jnp.concatenate(groups, axis=0).astype(BF16)

    def run(core):
        dots = jnp.zeros((1, rows), F32)
        tiles = copies(core)
        for index, (count, _) in enumerate(tiles):
            if index % 2 == 0:
                for _, copy in tiles[index : index + 2]:
                    copy.wait()
            first = core * half + starts[index]
            at = slice(starts[index], starts[index] + count)
            logits = lax.dot_general(
                held_ref[at, :], scaled, CONTRACT_LAST, preferred_element_type=F32
            )
            bias = jnp.broadcast_to(bias_ref[:, first : first + count], (LANES, count)).T
            logits = logits + jnp.concatenate([bias] * (rows // LANES), axis=1)
            top = jnp.max(logits, axis=0, keepdims=True)
            powers = jnp.exp(logits - top)
            powers_ref[at, :] = powers
            if count < sizes[index]:
                powers_ref[starts[index] + count : starts[index] + sizes[index], :] = jnp.zeros(
                    (sizes[index] - count, rows), F32
                )
            soft = mine_ref[at, :].astype(F32) + other_ref[at, :].astype(F32)
            stats_ref[index : index + 1, :] = top
            stats_ref[TILES + index : TILES + index + 1, :] = jnp.sum(
                powers, axis=0, keepdims=True
            )
            dots = dots + jnp.sum(soft * logits, axis=0, keepdims=True)
        dots_ref[...] = dots

    on_core(ids_ref[0], cores, run)


def grad_kernel(
    turn, starts, powers_ref, stats_ref, stats_far_ref, mass_ref, mass_far_ref, dots_ref,
    mine_ref, other_ref, first_ref, second_ref, loss_ref,
):
    stats, stats_far = stats_ref[...], stats_far_ref[...]
    tops, tops_far = stats[:TILES], stats_far[:TILES]
    top = jnp.maximum(
        jnp.max(tops, axis=0, keepdims=True), jnp.max(tops_far, axis=0, keepdims=True)
    )
    shrunk = jnp.exp(tops - top)
    terms = stats[TILES:] * shrunk + stats_far[TILES:] * jnp.exp(tops_far - top)
    total = jnp.sum(terms, axis=0, keepdims=True)
    mass = mass_ref[...] + mass_far_ref[...]
    scale = shrunk * (mass / total)
    for index, out_ref in ((turn, first_ref), (turn + TURNS, second_ref)):
        at = slice(starts[index], starts[index] + out_ref.shape[0])
        grad = powers_ref[at, :] * scale[index : index + 1]
        grad = grad - mine_ref[at, :].astype(F32) - other_ref[at, :].astype(F32)
        out_ref[...] = grad.astype(BF16)
    loss = 0.5 * mass * (top + jnp.log(total)) - dots_ref[...]
    loss_ref[...] = jnp.broadcast_to(jnp.sum(loss, axis=1, keepdims=True), loss_ref.shape)


def back_kernel(
    cores, tiling, ids_ref, weight_ref, normed_ref, loss_ref, live_ref, *refs
):
    grads, (out_ref, held_ref, arrived) = refs[:TILES], refs[TILES:]
    vocab, width = weight_ref.shape
    rows = normed_ref.shape[0]
    sizes, starts, half = tiling
    ones = jnp.ones((8, rows), BF16)

    def run(core):
        tiles = weight_copies(core, vocab, sizes, starts, half, weight_ref, held_ref, arrived)
        for _, copy in tiles:
            copy.start()
        for grad_ref, start, size in zip(grads, starts, sizes):
            sums = lax.dot_general(ones, grad_ref[...], CONTRACT_LAST, preferred_element_type=F32)
            out_ref[:, start : start + size] = sums[:1]
        total = None
        for grad_ref, start, (count, copy) in zip(grads, starts, tiles):
            copy.wait()
            term = lax.dot_general(
                grad_ref[:count, :], held_ref[start : start + count, :], CONTRACT_FIRST,
                preferred_element_type=F32,
            )
            total = term if total is None else total + term
        out_ref[:, half : half + width] = jnp.sum(total * normed_ref[...], axis=0, keepdims=True)

    on_core(ids_ref[0], cores, run)
    lane = lax.broadcasted_iota(jnp.int32, (1, LANES), 1)
    frames = jnp.sum(live_ref[...], axis=1, keepdims=True)
    out_ref[:, half + width :] = jnp.where(
        lane == 0, loss_ref[...], jnp.where(lane == 1, frames, 0.0)
    )


def term_kernel(near, ids_ref, own_ref, *refs):
    came, grads = refs[: 2 * (near - 1)], refs[2 * (near - 1) : 3 * near - 2]
    kept_ref, sent_ref, *halves = refs[3 * near - 2 :]
    count = kept_ref.shape[0]
    for index, half_ref in enumerate(halves):
        half_ref[ids_ref[1]] = came[2 * index][...]
        half_ref[1 - ids_ref[1]] = came[2 * index + 1][...]

    def product(side):
        rows = pl.ds(pl.multiple_of(side * count, count), count)
        total = None
        for state, grad in zip(
            [own_ref[rows, :]] + [half_ref[side] for half_ref in halves], grads
        ):
            term = lax.dot_general(state, grad[...], CONTRACT_LAST, preferred_element_type=F32)
            total = term if total is None else total + term
        return total

    sent_ref[...] = product(1 - ids_ref[0]).astype(BF16)
    kept_ref[...] = product(ids_ref[0])


def halve_kernel(parts, ids_ref, *refs):
    came, kept = refs[:parts], refs[parts : 2 * parts]
    kept_ref, sent_ref = refs[2 * parts :]
    count, width = kept_ref.shape
    width = width // parts
    for index in range(parts):
        at = slice(index * width, (index + 1) * width)

        def total(side):
            rows = pl.ds(pl.multiple_of(side * count, count), count)
            return kept[index][rows, :] + came[index][rows, :].astype(F32)

        sent_ref[:, at] = total(1 - ids_ref[0]).astype(BF16)
        kept_ref[:, at] = total(ids_ref[0])


def halve(bit, kept, came):
    count = kept[0].shape[0] // 2
    width = sum(part.shape[1] for part in kept)
    kept, sent = call(
        functools.partial(halve_kernel, len(kept)),
        bit[None],
        [*map(Pulled, came), *map(Pulled, kept)],
        [shape(count, width), shape(count, width, dtype=BF16)],
        8,
    )
    return kept, sent


def quarter_kernel(parts, ids_ref, *refs):
    came, kept, outs = refs[:parts], refs[parts : 2 * parts], refs[2 * parts :]
    count, width = outs[0].shape
    width = width // parts
    bit, core = ids_ref[0], ids_ref[1]
    for index in range(parts):
        at = slice(index * width, (index + 1) * width)
        for out_ref, chip_side, core_side in zip(
            outs, (bit, 1 - bit, bit, 1 - bit), (core, core, 1 - core, 1 - core)
        ):
            rows = pl.ds(pl.multiple_of((chip_side * 2 + core_side) * count, count), count)
            total = kept[index][rows, :] + came[index][rows, :].astype(F32)
            out_ref[:, at] = total.astype(out_ref.dtype)


def sum_kernel(*refs):
    total = refs[0][...]
    for ref in refs[1:-1]:
        total = total + ref[...]
    refs[-1][...] = total


def small_kernel(
    cores, half, width, ids_ref, near_ref, far_ref, gain_ref, bias_ref, loss_ref, scale_ref
):
    vocab = bias_ref.shape[1]
    tail, tail_far = near_ref[:, half + width :], far_ref[:, half + width :]
    inverse = 1.0 / tail[:, 1:2]
    near, far = near_ref[:, half : half + width], far_ref[:, half : half + width]
    gain_ref[...] = (near + far) * inverse
    loss_ref[...] = (tail + tail_far) * inverse
    scale_ref[...] = jnp.broadcast_to(inverse, scale_ref.shape)

    def run(core):
        low, high = (near_ref, far_ref) if core == 0 else (far_ref, near_ref)
        bias_ref[:, :half] = low[:, :half] * inverse
        bias_ref[:, half:] = high[:, : vocab - half] * inverse

    on_core(ids_ref[0], cores, run)


def finish_kernel(cores, tiling, ids_ref, scale_ref, *refs):
    parts, out_ref = refs[:-1], refs[-1]
    sizes, starts, half = tiling
    vocab = out_ref.shape[1]
    inverse = scale_ref[:, :1]

    def run(core):
        for turn in range(TURNS):
            kept, away, cross, far = parts[4 * turn : 4 * turn + 4]
            for owner, near_ref, came_ref in ((core, kept, away), (1 - core, cross, far)):
                total = (near_ref[...] + came_ref[...].astype(F32)) * inverse
                first = 0
                for index in (turn, turn + TURNS):
                    start = owner * half + starts[index]
                    count = max(0, min(sizes[index], vocab - start))
                    out_ref[:, start : start + count] = total[:, first : first + count]
                    first += sizes[index]

    on_core(ids_ref[0], cores, run)


def body(
    teacher_logits, routes, agreement, targets, lengths, student_hidden, out_weight, out_bias, gain
):
    cores = lax.axis_size("teach")
    chips = lax.axis_size("dp")
    devices = cores * chips
    rows = teacher_logits.shape[1]
    slots = cores * rows // devices
    vocab = teacher_logits.shape[2]
    width = student_hidden.shape[1]
    out_rows = width // devices
    size_a, size_b, size_c = torus_factors(chips)
    bits_a, bits_b, bits_c = bits_of(size_a), bits_of(size_b), bits_of(size_c)
    tiling = tile_plan(vocab, cores)
    sizes, starts, half = tiling
    core = lax.axis_index("teach").astype(jnp.int32)
    chip = lax.axis_index("dp").astype(jnp.int32)
    ids = core[None]
    exchange = [(i, 1 - i) for i in range(cores)]
    deep = [size_a * size_b << k for k in range(bits_c)]
    plans = (
        ((1, size_a), [size_a << k for k in range(bits_b)] + deep),
        ((size_a, size_b), [1 << k for k in range(bits_a)] + deep),
    )

    def swap(value):
        return lax.ppermute(value, "teach", exchange)

    def bit_of(stride):
        return (chip // stride) % 2

    def along(value, stride, size, step):
        return lax.ppermute(value, "dp", rotation(chips, stride, size, step))

    def flip(value, mask):
        return lax.ppermute(value, "dp", [(i, i ^ mask) for i in range(chips)])

    arrived = lax.all_to_all(
        student_hidden.reshape(chips, slots, width),
        "dp",
        split_axis=0,
        concat_axis=0,
        tiled=True,
    ).reshape(chips * slots, width)
    arrived_far = swap(arrived)

    dest_device = routes[:, 0]
    live_rows = live_mask(lengths, rows)
    mine, other, mass = call(
        functools.partial(soft_kernel, half, cores),
        ids,
        [
            teacher_logits[0].T,
            (0.5 * agreement.astype(F32) * live_rows)[None, :],
            (0.5 * live_rows)[None, :],
            targets[None, :],
        ],
        [shape(half, rows, dtype=BF16), shape(half, rows, dtype=BF16), shape(1, rows)],
        8,
        [pltpu.VMEM((vocab, rows), F32)],
    )
    other = swap(other)
    mass_far = swap(mass)

    place = (dest_device % chips) * slots + route_slots(dest_device)
    place = jnp.where(dest_device // chips == core, place, place + chips * slots)
    near_ids = [(chip // stride) % size for (stride, size), _ in plans]
    weight = in_hbm(out_weight.T)
    held = [pltpu.VMEM((half, width), BF16), pltpu.SemaphoreType.DMA((TILES,))]
    normed, powers, stats, dots, *own_states = call(
        functools.partial(student_kernel, cores, chips, plans, tiling),
        jnp.stack([core, *near_ids]),
        [weight, place[None, :], arrived, arrived_far, gain[None, :], out_bias[None, :], mine, other],
        [shape(rows, width), shape(half, rows), shape(2 * TILES, rows), shape(1, rows)]
        + [
            shape(width // size // (2 if step else 1), rows, dtype=BF16)
            for (_, size), _ in plans
            for step in range(size)
        ],
        24,
        [pltpu.VMEM((width, rows), F32), *held],
        fetched=1,
    )
    stats_far = swap(stats)
    states = []
    for (stride, size), _ in plans:
        group = [own_states[0]]
        for step in range(1, size):
            direct = along(own_states[step], stride, size, step)
            group += [direct, swap(direct)]
        states.append(group)
        own_states = own_states[size:]

    grads = [None] * TILES
    for turn in range(TURNS):
        grads[turn], grads[turn + TURNS], loss = call(
            functools.partial(grad_kernel, turn, starts),
            None,
            [powers, stats, stats_far, mass, mass_far, dots, mine, other],
            [shape(sizes[turn], rows, dtype=BF16)] * 2 + [shape(1, LANES)],
            6,
        )

    gathered = {}
    for turn in range(TURNS):
        for side, ((stride, size), _) in enumerate(plans):
            grad = grads[turn + TURNS * side]
            gathered[turn, side] = [
                along(grad, stride, size, step) if step else grad for step in range(size)
            ]

    ends = []
    for turn in range(TURNS):
        kept, came = [], []
        for side, ((_, size), strides) in enumerate(plans):
            count = width // size // 2
            part, sent = call(
                functools.partial(term_kernel, size),
                jnp.stack([bit_of(strides[0]), core]),
                [*states[side], *gathered[turn, side]],
                [shape(count, sizes[turn]), shape(count, sizes[turn], dtype=BF16)],
                8,
                [pltpu.VMEM((2, count, rows), BF16)] * (size - 1),
            )
            for depth, stride in enumerate(strides[: len(strides) - bits_c]):
                if depth:
                    part, sent = halve(bit_of(stride), [part], [got])
                got = in_hbm(flip(sent, stride))
            kept.append(part)
            came.append(got)
        for stride in deep[:-1]:
            part, sent = halve(bit_of(stride), kept, came)
            kept, came = [part], [flip(sent, stride)]
        width_here = sum(part.shape[1] for part in kept)
        part, away, cross, far = call(
            functools.partial(quarter_kernel, len(kept)),
            jnp.stack([bit_of(deep[-1]), core]),
            [*map(Pulled, came), *map(Pulled, kept)],
            [
                shape(out_rows, width_here),
                shape(out_rows, width_here, dtype=BF16),
                shape(out_rows, width_here),
                shape(out_rows, width_here, dtype=BF16),
            ],
            8,
        )
        away = flip(away, deep[-1])
        pairs = [
            (c * chips + i, (1 - c) * chips + (i ^ deep[-1]))
            for c in range(cores)
            for i in range(chips)
        ]
        far = lax.ppermute(far, ("teach", "dp"), pairs)
        cross = swap(cross)
        ends += [part, away, cross, far]

    small = call(
        functools.partial(back_kernel, cores, tiling),
        ids,
        [weight, normed, loss, live_rows[None, :], *grads],
        shape(1, half + width + LANES),
        16,
        held,
        fetched=1,
    )
    for stride in deep + [1 << k for k in range(bits_a + bits_b)]:
        got = flip(small, stride)
        small = call(sum_kernel, None, [small, got], shape(*small.shape), 2)
    small_far = swap(small)
    gain_sum, bias_sum, loss_sum, scale = call(
        functools.partial(small_kernel, cores, half, width),
        ids,
        [small, small_far],
        [shape(1, width), shape(1, vocab), shape(1, LANES), shape(1, LANES)],
        2,
    )

    weight_grad = call(
        functools.partial(finish_kernel, cores, tiling),
        ids,
        [scale, *map(Pulled, ends)],
        shape(out_rows, vocab),
        8,
    )
    return (weight_grad, gain_sum[0], bias_sum[0], loss_sum[0, 0])


def solution(mesh):
    return jax.shard_map(
        body,
        mesh=mesh,
        in_specs=(
            P("teach", "dp", None),
            P("dp", None),
            P("dp"),
            P("dp"),
            P("dp"),
            P(("teach", "dp"), None),
            P(),
            P(),
            P(),
        ),
        out_specs=(P(("teach", "dp"), None), P(), P(), P()),
        check_vma=False,
    )
```

```python
import functools
import math

import jax
import jax.numpy as jnp
from jax import lax
from jax.experimental import pallas as pl
from jax.experimental.pallas import tpu as pltpu
from jax.sharding import PartitionSpec as P


LMAX = 256
EPSILON = 1e-05
LANES = 128
TURNS = 2
TILES = 2 * TURNS
F32 = jnp.float32
BF16 = jnp.bfloat16
CONTRACT_LAST = (((1,), (1,)), ((), ()))
CONTRACT_FIRST = (((0,), (0,)), ((), ()))


def bits_of(count):
    return count.bit_length() - 1


def torus_factors(count):
    bits = bits_of(count)
    small = bits // 3
    middle = (bits - small) // 2
    return 1 << small, 1 << middle, 1 << (bits - small - middle)


def rotation(count, stride, size, step):
    def moved(index):
        place = (index // stride) % size
        return index + ((place + step) % size - place) * stride

    return [(index, moved(index)) for index in range(count)]


def tile_plan(vocab, cores):
    groups = -(-vocab // (2 * cores * LANES))
    sizes = [(groups + turn) // TURNS * LANES for turn in range(TURNS)]
    starts = [0]
    for size in sizes * 2:
        starts.append(starts[-1] + size)
    return sizes * 2, starts[:-1], starts[-1]


def route_slots(dest_device):
    row_ids = jnp.arange(dest_device.shape[0], dtype=jnp.int32)
    same = (dest_device[:, None] == dest_device[None, :]) & (row_ids[:, None] < row_ids[None, :])
    return jnp.sum(same.astype(jnp.int32), axis=0)


def live_mask(lengths_block, row_total):
    row_ids = jnp.arange(row_total, dtype=jnp.int32)
    utterance = row_ids // LMAX
    frame_pos = row_ids % LMAX
    picks = utterance[None, :] == jnp.arange(lengths_block.shape[0], dtype=jnp.int32)[:, None]
    row_length = jnp.sum(jnp.where(picks, lengths_block[:, None], 0), axis=0)
    return (frame_pos < row_length).astype(F32)


def shape(*dims, dtype=F32):
    return jax.ShapeDtypeStruct(dims, dtype)


class Pulled:
    def __init__(self, value):
        self.value = value


def call(kernel, scalars, arrays, out_shape, grant, scratch=(), fetched=0):
    operands, in_specs, pulled = [], [], []
    if scalars is not None:
        operands.append(scalars)
        in_specs.append(pl.BlockSpec(memory_space=pltpu.SMEM))
    lead = len(operands)
    for index, array in enumerate(arrays):
        space = pltpu.VMEM
        if isinstance(array, Pulled):
            array, space = array.value, pl.ANY
            pulled.append(lead + index)
        elif index < fetched:
            space = pltpu.HBM
        operands.append(array)
        in_specs.append(pl.BlockSpec(memory_space=space))
    buffers = [pltpu.VMEM(operands[index].shape, operands[index].dtype) for index in pulled]
    if pulled:
        buffers.append(pltpu.SemaphoreType.DMA((len(pulled),)))

    def run(*refs):
        refs = list(refs)
        if pulled:
            held, arrived = refs[-len(buffers) : -1], refs[-1]
            refs = refs[: -len(buffers)]
            copies = [
                pltpu.make_async_copy(refs[index], buffer, arrived.at[place])
                for place, (index, buffer) in enumerate(zip(pulled, held))
            ]
            for copy in copies:
                copy.start()
            for copy in copies:
                copy.wait()
            for index, buffer in zip(pulled, held):
                refs[index] = buffer
        kernel(*refs)

    return pl.pallas_call(
        run,
        in_specs=in_specs,
        out_specs=jax.tree.map(lambda _: pl.BlockSpec(memory_space=pltpu.VMEM), out_shape),
        out_shape=out_shape,
        scratch_shapes=list(scratch) + buffers,
        compiler_params=pltpu.CompilerParams(vmem_limit_bytes=grant << 20),
    )(*operands)


def in_hbm(value):
    return pltpu.with_memory_space_constraint(value, pltpu.HBM)


def on_core(core, cores, run):
    for index in range(cores):
        pl.when(core == index)(functools.partial(run, index))


def soft_kernel(half, cores, ids_ref, logits_ref, weight_ref, hot_ref, target_ref, mine_ref, other_ref, mass_ref, powers_ref):
    vocab, rows = logits_ref.shape
    block = math.gcd(half, vocab - half)

    def rows_at(index):
        return pl.ds(pl.multiple_of(index * block, block), block)

    def highest(index, top):
        values = logits_ref[rows_at(index), :].astype(F32)
        return jnp.maximum(top, jnp.max(values, axis=0, keepdims=True))

    top = lax.fori_loop(
        0, vocab // block, highest, jnp.full((1, rows), -jnp.inf, F32), unroll=5
    )

    def raised(index, total):
        powers = jnp.exp(logits_ref[rows_at(index), :].astype(F32) - top)
        powers_ref[rows_at(index), :] = powers
        return total + jnp.sum(powers, axis=0, keepdims=True)

    total = lax.fori_loop(0, vocab // block, raised, jnp.zeros((1, rows), F32), unroll=5)
    scale = weight_ref[...] / total
    hot = hot_ref[...]
    places = lax.broadcasted_iota(jnp.int32, (block, rows), 0)

    def write(out_ref, start, count, mass):
        def one(index, mass):
            at = index * block + start
            soft = powers_ref[pl.ds(pl.multiple_of(at, block), block), :] * scale
            soft = soft + jnp.where(places + at == target_ref[...], hot, 0.0)
            soft = soft.astype(BF16)
            out_ref[rows_at(index), :] = soft
            return mass + jnp.sum(soft.astype(F32), axis=0, keepdims=True)

        return lax.fori_loop(0, count // block, one, mass, unroll=4)

    def run(core):
        refs = (mine_ref, other_ref)
        low_ref, high_ref = refs if core == 0 else refs[::-1]
        mass = write(low_ref, 0, half, jnp.zeros((1, rows), F32))
        mass_ref[...] = write(high_ref, half, vocab - half, mass)
        high_ref[vocab - half :, :] = jnp.zeros((2 * half - vocab, rows), BF16)

    on_core(ids_ref[0], cores, run)


def weight_copies(core, vocab, sizes, starts, half, weight_ref, held_ref, arrived):
    tiles = []
    for index, (size, start) in enumerate(zip(sizes, starts)):
        first = core * half + start
        count = max(0, min(size, vocab - first))
        copy = pltpu.make_async_copy(
            weight_ref.at[pl.ds(first, count), :],
            held_ref.at[pl.ds(start, count), :],
            arrived.at[index],
        )
        tiles.append((count, copy))
    return tiles


def student_kernel(
    cores, chips, plans, tiling, ids_ref, weight_ref, place_ref, near_ref, far_ref, gain_ref,
    bias_ref, mine_ref, other_ref, normed_ref, powers_ref, stats_ref, dots_ref, *refs,
):
    state_refs, (turned_ref, held_ref, arrived) = refs[:-3], refs[-3:]
    rows = place_ref.shape[1]
    count = near_ref.shape[0]
    vocab, width = weight_ref.shape
    block = width // (cores * chips)
    sizes, starts, half = tiling

    def copies(core):
        return weight_copies(core, vocab, sizes, starts, half, weight_ref, held_ref, arrived)

    def fetch(tiles, core):
        for _, copy in copies(core)[tiles]:
            copy.start()

    on_core(ids_ref[0], cores, functools.partial(fetch, slice(0, 2)))
    ids = lax.broadcasted_iota(jnp.int32, (count, rows), 0)
    place = place_ref[...]

    def taken(hit, states_ref):
        return lax.dot_general(
            hit.astype(F32).astype(BF16),
            states_ref[...],
            CONTRACT_FIRST,
            preferred_element_type=F32,
        )

    hidden = taken(place == ids, near_ref) + taken(place - count == ids, far_ref)
    on_core(ids_ref[0], cores, functools.partial(fetch, slice(2, None)))
    centre = jnp.mean(hidden, axis=1, keepdims=True)
    moved = hidden - centre
    spread = jnp.mean(moved * moved, axis=1, keepdims=True)
    normed = moved * lax.rsqrt(spread + EPSILON)
    normed_ref[...] = normed
    scaled = normed * gain_ref[...]
    turned_ref[...] = scaled.T
    scaled = scaled.astype(BF16)
    refs = iter(state_refs)
    for side, ((stride, size), strides) in enumerate(plans):
        for step in range(size):
            to_near = lax.rem(ids_ref[1 + side] + step, size) * stride
            places = [0]
            for far in strides[1:] if step else strides:
                places = [at + bit * far for at in places for bit in (0, 1)]
            if step:
                to_near = to_near + ids_ref[0] * strides[0]
            groups = []
            for at in places:
                for core in range(cores):
                    first = (core * chips + at + to_near) * block
                    groups.append(turned_ref[pl.ds(pl.multiple_of(first, block), block), :])
            next(refs)[...] = jnp.concatenate(groups, axis=0).astype(BF16)

    def run(core):
        dots = jnp.zeros((1, rows), F32)
        tiles = copies(core)
        for index, (count, _) in enumerate(tiles):
            if index % 2 == 0:
                for _, copy in tiles[index : index + 2]:
                    copy.wait()
            first = core * half + starts[index]
            at = slice(starts[index], starts[index] + count)
            logits = lax.dot_general(
                held_ref[at, :], scaled, CONTRACT_LAST, preferred_element_type=F32
            )
            bias = jnp.broadcast_to(bias_ref[:, first : first + count], (LANES, count)).T
            logits = logits + jnp.concatenate([bias] * (rows // LANES), axis=1)
            top = jnp.max(logits, axis=0, keepdims=True)
            powers = jnp.exp(logits - top)
            powers_ref[at, :] = powers
            if count < sizes[index]:
                powers_ref[starts[index] + count : starts[index] + sizes[index], :] = jnp.zeros(
                    (sizes[index] - count, rows), F32
                )
            soft = mine_ref[at, :].astype(F32) + other_ref[at, :].astype(F32)
            stats_ref[index : index + 1, :] = top
            stats_ref[TILES + index : TILES + index + 1, :] = jnp.sum(
                powers, axis=0, keepdims=True
            )
            dots = dots + jnp.sum(soft * logits, axis=0, keepdims=True)
        dots_ref[...] = dots

    on_core(ids_ref[0], cores, run)


def grad_kernel(
    turn, starts, powers_ref, stats_ref, stats_far_ref, mass_ref, mass_far_ref, dots_ref,
    mine_ref, other_ref, first_ref, second_ref, loss_ref,
):
    stats, stats_far = stats_ref[...], stats_far_ref[...]
    tops, tops_far = stats[:TILES], stats_far[:TILES]
    top = jnp.maximum(
        jnp.max(tops, axis=0, keepdims=True), jnp.max(tops_far, axis=0, keepdims=True)
    )
    shrunk = jnp.exp(tops - top)
    terms = stats[TILES:] * shrunk + stats_far[TILES:] * jnp.exp(tops_far - top)
    total = jnp.sum(terms, axis=0, keepdims=True)
    mass = mass_ref[...] + mass_far_ref[...]
    scale = shrunk * (mass / total)
    for index, out_ref in ((turn, first_ref), (turn + TURNS, second_ref)):
        at = slice(starts[index], starts[index] + out_ref.shape[0])
        grad = powers_ref[at, :] * scale[index : index + 1]
        grad = grad - mine_ref[at, :].astype(F32) - other_ref[at, :].astype(F32)
        out_ref[...] = grad.astype(BF16)
    loss = 0.5 * mass * (top + jnp.log(total)) - dots_ref[...]
    loss_ref[...] = jnp.broadcast_to(jnp.sum(loss, axis=1, keepdims=True), loss_ref.shape)


def back_kernel(
    cores, tiling, ids_ref, weight_ref, normed_ref, loss_ref, live_ref, *refs
):
    grads, (out_ref, held_ref, arrived) = refs[:TILES], refs[TILES:]
    vocab, width = weight_ref.shape
    rows = normed_ref.shape[0]
    sizes, starts, half = tiling
    ones = jnp.ones((8, rows), BF16)

    def run(core):
        tiles = weight_copies(core, vocab, sizes, starts, half, weight_ref, held_ref, arrived)
        for _, copy in tiles:
            copy.start()
        for grad_ref, start, size in zip(grads, starts, sizes):
            sums = lax.dot_general(ones, grad_ref[...], CONTRACT_LAST, preferred_element_type=F32)
            out_ref[:, start : start + size] = sums[:1]
        total = None
        for grad_ref, start, (count, copy) in zip(grads, starts, tiles):
            copy.wait()
            term = lax.dot_general(
                grad_ref[:count, :], held_ref[start : start + count, :], CONTRACT_FIRST,
                preferred_element_type=F32,
            )
            total = term if total is None else total + term
        out_ref[:, half : half + width] = jnp.sum(total * normed_ref[...], axis=0, keepdims=True)

    on_core(ids_ref[0], cores, run)
    lane = lax.broadcasted_iota(jnp.int32, (1, LANES), 1)
    frames = jnp.sum(live_ref[...], axis=1, keepdims=True)
    out_ref[:, half + width :] = jnp.where(
        lane == 0, loss_ref[...], jnp.where(lane == 1, frames, 0.0)
    )


def term_kernel(near, ids_ref, own_ref, *refs):
    came, grads = refs[: 2 * (near - 1)], refs[2 * (near - 1) : 3 * near - 2]
    kept_ref, sent_ref, *halves = refs[3 * near - 2 :]
    count = kept_ref.shape[0]
    for index, half_ref in enumerate(halves):
        half_ref[ids_ref[1]] = came[2 * index][...]
        half_ref[1 - ids_ref[1]] = came[2 * index + 1][...]

    def product(side):
        rows = pl.ds(pl.multiple_of(side * count, count), count)
        total = None
        for state, grad in zip(
            [own_ref[rows, :]] + [half_ref[side] for half_ref in halves], grads
        ):
            term = lax.dot_general(state, grad[...], CONTRACT_LAST, preferred_element_type=F32)
            total = term if total is None else total + term
        return total

    sent_ref[...] = product(1 - ids_ref[0]).astype(BF16)
    kept_ref[...] = product(ids_ref[0])


def halve_kernel(parts, ids_ref, *refs):
    came, kept = refs[:parts], refs[parts : 2 * parts]
    kept_ref, sent_ref = refs[2 * parts :]
    count, width = kept_ref.shape
    width = width // parts
    for index in range(parts):
        at = slice(index * width, (index + 1) * width)

        def total(side):
            rows = pl.ds(pl.multiple_of(side * count, count), count)
            return kept[index][rows, :] + came[index][rows, :].astype(F32)

        sent_ref[:, at] = total(1 - ids_ref[0]).astype(BF16)
        kept_ref[:, at] = total(ids_ref[0])


def halve(bit, kept, came):
    count = kept[0].shape[0] // 2
    width = sum(part.shape[1] for part in kept)
    kept, sent = call(
        functools.partial(halve_kernel, len(kept)),
        bit[None],
        [*map(Pulled, came), *map(Pulled, kept)],
        [shape(count, width), shape(count, width, dtype=BF16)],
        8,
    )
    return kept, sent


def quarter_kernel(parts, ids_ref, *refs):
    came, kept, outs = refs[:parts], refs[parts : 2 * parts], refs[2 * parts :]
    count, width = outs[0].shape
    width = width // parts
    bit, core = ids_ref[0], ids_ref[1]
    for index in range(parts):
        at = slice(index * width, (index + 1) * width)
        for out_ref, chip_side, core_side in zip(
            outs, (bit, 1 - bit, bit, 1 - bit), (core, core, 1 - core, 1 - core)
        ):
            rows = pl.ds(pl.multiple_of((chip_side * 2 + core_side) * count, count), count)
            total = kept[index][rows, :] + came[index][rows, :].astype(F32)
            out_ref[:, at] = total.astype(out_ref.dtype)


def sum_kernel(*refs):
    total = refs[0][...]
    for ref in refs[1:-1]:
        total = total + ref[...]
    refs[-1][...] = total


def small_kernel(
    cores, half, width, ids_ref, near_ref, far_ref, gain_ref, bias_ref, loss_ref, scale_ref
):
    vocab = bias_ref.shape[1]
    tail, tail_far = near_ref[:, half + width :], far_ref[:, half + width :]
    inverse = 1.0 / tail[:, 1:2]
    near, far = near_ref[:, half : half + width], far_ref[:, half : half + width]
    gain_ref[...] = (near + far) * inverse
    loss_ref[...] = (tail + tail_far) * inverse
    scale_ref[...] = jnp.broadcast_to(inverse, scale_ref.shape)

    def run(core):
        low, high = (near_ref, far_ref) if core == 0 else (far_ref, near_ref)
        bias_ref[:, :half] = low[:, :half] * inverse
        bias_ref[:, half:] = high[:, : vocab - half] * inverse

    on_core(ids_ref[0], cores, run)


def join_kernel(kept_ref, away_ref, cross_ref, far_ref, own_ref, other_ref):
    own_ref[...] = kept_ref[...] + away_ref[...].astype(F32)
    other_ref[...] = cross_ref[...] + far_ref[...].astype(F32)


def finish_kernel(cores, tiling, ids_ref, scale_ref, *refs):
    parts, out_ref = refs[:-1], refs[-1]
    sizes, starts, half = tiling
    vocab = out_ref.shape[1]
    inverse = scale_ref[:, :1]

    def run(core):
        for turn in range(TURNS):
            if turn < TURNS - 1:
                sums = [ref[...] for ref in parts[2 * turn : 2 * turn + 2]]
            else:
                kept, away, cross, far = parts[2 * turn :]
                sums = [
                    kept[...] + away[...].astype(F32),
                    cross[...] + far[...].astype(F32),
                ]
            for owner, total in zip((core, 1 - core), sums):
                total = total * inverse
                first = 0
                for index in (turn, turn + TURNS):
                    start = owner * half + starts[index]
                    count = max(0, min(sizes[index], vocab - start))
                    out_ref[:, start : start + count] = total[:, first : first + count]
                    first += sizes[index]

    on_core(ids_ref[0], cores, run)


def body(
    teacher_logits, routes, agreement, targets, lengths, student_hidden, out_weight, out_bias, gain
):
    cores = lax.axis_size("teach")
    chips = lax.axis_size("dp")
    devices = cores * chips
    rows = teacher_logits.shape[1]
    slots = cores * rows // devices
    vocab = teacher_logits.shape[2]
    width = student_hidden.shape[1]
    out_rows = width // devices
    size_a, size_b, size_c = torus_factors(chips)
    bits_a, bits_b, bits_c = bits_of(size_a), bits_of(size_b), bits_of(size_c)
    tiling = tile_plan(vocab, cores)
    sizes, starts, half = tiling
    core = lax.axis_index("teach").astype(jnp.int32)
    chip = lax.axis_index("dp").astype(jnp.int32)
    ids = core[None]
    exchange = [(i, 1 - i) for i in range(cores)]
    deep = [size_a * size_b << k for k in range(bits_c)]
    plans = (
        ((1, size_a), [size_a << k for k in range(bits_b)] + deep),
        ((size_a, size_b), [1 << k for k in range(bits_a)] + deep),
    )

    def swap(value):
        return lax.ppermute(value, "teach", exchange)

    def bit_of(stride):
        return (chip // stride) % 2

    def along(value, stride, size, step):
        return lax.ppermute(value, "dp", rotation(chips, stride, size, step))

    def flip(value, mask):
        return lax.ppermute(value, "dp", [(i, i ^ mask) for i in range(chips)])

    arrived = lax.all_to_all(
        student_hidden.reshape(chips, slots, width),
        "dp",
        split_axis=0,
        concat_axis=0,
        tiled=True,
    ).reshape(chips * slots, width)
    arrived_far = swap(arrived)

    dest_device = routes[:, 0]
    live_rows = live_mask(lengths, rows)
    mine, other, mass = call(
        functools.partial(soft_kernel, half, cores),
        ids,
        [
            teacher_logits[0].T,
            (0.5 * agreement.astype(F32) * live_rows)[None, :],
            (0.5 * live_rows)[None, :],
            targets[None, :],
        ],
        [shape(half, rows, dtype=BF16), shape(half, rows, dtype=BF16), shape(1, rows)],
        8,
        [pltpu.VMEM((vocab, rows), F32)],
    )
    other = swap(other)
    mass_far = swap(mass)

    place = (dest_device % chips) * slots + route_slots(dest_device)
    place = jnp.where(dest_device // chips == core, place, place + chips * slots)
    near_ids = [(chip // stride) % size for (stride, size), _ in plans]
    weight = in_hbm(out_weight.T)
    held = [pltpu.VMEM((half, width), BF16), pltpu.SemaphoreType.DMA((TILES,))]
    normed, powers, stats, dots, *own_states = call(
        functools.partial(student_kernel, cores, chips, plans, tiling),
        jnp.stack([core, *near_ids]),
        [weight, place[None, :], arrived, arrived_far, gain[None, :], out_bias[None, :], mine, other],
        [shape(rows, width), shape(half, rows), shape(2 * TILES, rows), shape(1, rows)]
        + [
            shape(width // size // (2 if step else 1), rows, dtype=BF16)
            for (_, size), _ in plans
            for step in range(size)
        ],
        24,
        [pltpu.VMEM((width, rows), F32), *held],
        fetched=1,
    )
    stats_far = swap(stats)
    states = []
    for (stride, size), _ in plans:
        group = [own_states[0]]
        for step in range(1, size):
            direct = along(own_states[step], stride, size, step)
            group += [direct, swap(direct)]
        states.append(group)
        own_states = own_states[size:]

    grads = [None] * TILES
    for turn in range(TURNS):
        grads[turn], grads[turn + TURNS], loss = call(
            functools.partial(grad_kernel, turn, starts),
            None,
            [powers, stats, stats_far, mass, mass_far, dots, mine, other],
            [shape(sizes[turn], rows, dtype=BF16)] * 2 + [shape(1, LANES)],
            6,
        )

    gathered = {}
    for turn in range(TURNS):
        for side, ((stride, size), _) in enumerate(plans):
            grad = grads[turn + TURNS * side]
            gathered[turn, side] = [
                along(grad, stride, size, step) if step else grad for step in range(size)
            ]

    ends = []
    for turn in range(TURNS):
        kept, came = [], []
        for side, ((_, size), strides) in enumerate(plans):
            count = width // size // 2
            part, sent = call(
                functools.partial(term_kernel, size),
                jnp.stack([bit_of(strides[0]), core]),
                [*states[side], *gathered[turn, side]],
                [shape(count, sizes[turn]), shape(count, sizes[turn], dtype=BF16)],
                8,
                [pltpu.VMEM((2, count, rows), BF16)] * (size - 1),
            )
            for depth, stride in enumerate(strides[: len(strides) - bits_c]):
                if depth:
                    part, sent = halve(bit_of(stride), [part], [got])
                got = in_hbm(flip(sent, stride))
            kept.append(part)
            came.append(got)
        for stride in deep[:-1]:
            part, sent = halve(bit_of(stride), kept, came)
            kept, came = [part], [flip(sent, stride)]
        width_here = sum(part.shape[1] for part in kept)
        part, away, cross, far = call(
            functools.partial(quarter_kernel, len(kept)),
            jnp.stack([bit_of(deep[-1]), core]),
            [*map(Pulled, came), *map(Pulled, kept)],
            [
                shape(out_rows, width_here),
                shape(out_rows, width_here, dtype=BF16),
                shape(out_rows, width_here),
                shape(out_rows, width_here, dtype=BF16),
            ],
            8,
        )
        away = flip(away, deep[-1])
        pairs = [
            (c * chips + i, (1 - c) * chips + (i ^ deep[-1]))
            for c in range(cores)
            for i in range(chips)
        ]
        far = lax.ppermute(far, ("teach", "dp"), pairs)
        cross = swap(cross)
        if turn < TURNS - 1:
            ends += call(
                join_kernel,
                None,
                [*map(Pulled, (part, away, cross, far))],
                [shape(out_rows, width_here)] * 2,
                4,
            )
        else:
            ends += [part, away, cross, far]

    small = call(
        functools.partial(back_kernel, cores, tiling),
        ids,
        [weight, normed, loss, live_rows[None, :], *grads],
        shape(1, half + width + LANES),
        16,
        held,
        fetched=1,
    )
    for stride in deep + [1 << k for k in range(bits_a + bits_b)]:
        got = flip(small, stride)
        small = call(sum_kernel, None, [small, got], shape(*small.shape), 2)
    small_far = swap(small)
    gain_sum, bias_sum, loss_sum, scale = call(
        functools.partial(small_kernel, cores, half, width),
        ids,
        [small, small_far],
        [shape(1, width), shape(1, vocab), shape(1, LANES), shape(1, LANES)],
        2,
    )

    weight_grad = call(
        functools.partial(finish_kernel, cores, tiling),
        ids,
        [scale, *map(Pulled, ends)],
        shape(out_rows, vocab),
        8,
    )
    return (weight_grad, gain_sum[0], bias_sum[0], loss_sum[0, 0])


def solution(mesh):
    return jax.shard_map(
        body,
        mesh=mesh,
        in_specs=(
            P("teach", "dp", None),
            P("dp", None),
            P("dp"),
            P("dp"),
            P("dp"),
            P(("teach", "dp"), None),
            P(),
            P(),
            P(),
        ),
        out_specs=(P(("teach", "dp"), None), P(), P(), P()),
        check_vma=False,
    )
```
